256 devices in a mesh: mod: 2 (over core), seq: 8 (over z), tp: 16 (over x, y).
Axes of the slice: x: 4, y: 4, z: 8, core: 2. Of those that a mesh axis runs over, the one named last changes fastest.
Arguments:
- tokens: bfloat16 [8192, 4096], P(('mod', 'seq'), 'tp'), may hold values from -6 to 6
- modality: int32 [8192], replicated, may hold values from 0 to 1, as said below
- norm_gain: float32 [2, 4096], replicated, may hold values from 0.1 to 1.9
- input_weight: bfloat16 [2, 4096, 3, 4096], P('mod', None, None, 'tp'), may hold values from -0.09375 to 0.09375
- head_gain: float32 [2, 2, 128], replicated, may hold values from 1 to 2
- output_weight: bfloat16 [2, 4096, 4096], P('mod', 'tp'), may hold values from -0.125 to 0.125
Outputs:
- update: bfloat16 [8192, 4096], P(('mod', 'seq'), 'tp')
The draws below stay inside these ranges and needn't reach their ends.
Inputs may be any that keep to these rules, and one draw needn't show every extreme that they name: Each value is constant over aligned spans of 64 tokens. Each token shard (the 512 tokens of one index of mod+seq) holds between 3 and 5 image spans, so at most 320 tokens of either modality. In every draw, for some index of seq both of its token shards hold 320 text tokens, and for another index of seq both hold 320 image tokens.
All inputs are finite; a program needn't handle non-finite values.
Results may differ from the reference program's by a relative error of at most 0.019.
Values may be sent and summed in bfloat16 or wider, within the bound.
A program may use at most 192 MiB of HBM per device.

```python
import math
import jax
import jax.numpy as jnp
from jax import lax

D = 4096
HEADS = 32
HD = 128
TOK_DEV = 512
SPAN = 64
TOKENS = 8192
N_MOD = 2
N_SEQ = 8
N_TP = 16


def draw_modality(key, part):
    shards = TOKENS // TOK_DEV
    blocks = TOK_DEV // SPAN
    key_count, key_seq, key_side, key_rank = jax.random.split(key, 4)
    image_blocks = jax.random.randint(key_count, (N_MOD, N_SEQ), 3, blocks - 2)
    seq_pick = jax.random.permutation(key_seq, N_SEQ)
    side = jax.random.randint(key_side, (), 0, 2)
    first_count = jnp.where(side == 1, blocks - 3, 3)
    second_count = blocks - first_count
    image_blocks = image_blocks.at[:, seq_pick[0]].set(first_count)
    image_blocks = image_blocks.at[:, seq_pick[1]].set(second_count)
    counts = image_blocks.reshape(shards)
    priority = jax.random.randint(key_rank, (shards, blocks), 0, 1 << 20) * blocks + jnp.arange(blocks, dtype=jnp.int32)[None, :]
    ranking = jnp.argsort(jnp.argsort(priority, axis=1), axis=1)
    is_image = (ranking < counts[:, None]).astype(jnp.int32)
    return jnp.repeat(is_image, SPAN, axis=1).reshape(TOKENS)


def strengthened(array, stream_key, source, target, parts, factor):
    owner, partner = [(jnp.arange(array.shape[position]) // (array.shape[position] // parts)).reshape([-1 if axis == position else 1 for axis in range(array.ndim)]) for position in (source, target)]
    chosen = jax.random.permutation(stream_key, parts)[partner]
    strong = (owner == chosen) | (owner == (partner + parts // 2) % parts)
    return jnp.where(strong, factor * array, array)


def steps_of(stream_key, dims, pieces, smallest, top_value):
    level, own = 1.0, jax.random.fold_in(stream_key, 6)
    for axis_at, shards_of in pieces:
        heights = jnp.exp(jax.random.uniform(jax.random.fold_in(own, axis_at), (shards_of,), jnp.float32, smallest / len(pieces), top_value / len(pieces)))
        level = level * jnp.repeat(heights, dims[axis_at] // shards_of).reshape([-1 if axis == axis_at else 1 for axis in range(len(dims))])
    return level


def centred(own_key, extent, deviation, reach, pieces=(), kind=jnp.bfloat16):
    level = steps_of(own_key, extent, pieces, -0.22, 0.18) if pieces else 1.0
    drawn = jax.random.normal(own_key, extent, jnp.float32) * deviation * level
    return jnp.minimum(jnp.maximum(drawn, -reach), reach).astype(kind)


def bell_draw_with(stream_key, dims, width, reach, cuts, heavy, kind=jnp.bfloat16):
    result = width * jax.random.normal(stream_key, dims, jnp.float32)
    if cuts:
        result = result * steps_of(stream_key, dims, cuts, -0.22, 0.18)
    return jnp.clip(strengthened(result, jax.random.fold_in(stream_key, 3), *heavy), -reach, reach).astype(kind)


def setup_inputs(seed: int = 0) -> dict:
    splits = jax.random.split(jax.random.key(seed), 7)
    return {
        "tokens": centred(splits[0], (TOKENS, D), 1.0, 6.0, ((0, 16), (1, 16))),
        "modality": draw_modality(jax.random.fold_in(splits[6], 71), 0),
        "norm_gain": jnp.clip(1.0 + 0.18 * jax.random.normal(splits[2], (2, D), jnp.float32), 0.1, 1.9),
        "input_weight": centred(splits[3], (2, D, 3, D), D ** -0.5, 0.09375, ((0, 2), (3, 16))),
        "head_gain": jnp.clip(jax.random.uniform(splits[4], (2, 2, HD), jnp.float32, 1.0, 2.0), 1.0, 2.0),
        "output_weight": bell_draw_with(splits[5], (2, D, D), D ** -0.5, 0.125, ((0, 2), (1, 16)), (1, 2, 16, 2.0)),
    }


epsilon = 1e-05

def head_norm(part, gain):
    return part * lax.rsqrt(lax.optimization_barrier(jnp.mean(part * part, axis=-1, keepdims=True)) + epsilon) * gain

def reference(tokens, modality, norm_gain, input_weight, head_gain, output_weight):
    image = (modality == 1)[:, None]
    states = tokens.astype(jnp.float32)
    gain = jnp.where(image, norm_gain[1][None, :], norm_gain[0][None, :])
    normed = (states * lax.rsqrt(lax.optimization_barrier(jnp.mean(states * states, axis=1, keepdims=True)) + epsilon) * gain).astype(jnp.bfloat16)
    text_part = jnp.dot(normed, input_weight[0].reshape(D, 3 * D), preferred_element_type=jnp.float32)
    image_part = jnp.dot(normed, input_weight[1].reshape(D, 3 * D), preferred_element_type=jnp.float32)
    projected = jnp.where(image, image_part, text_part).reshape(TOKENS, 3, HEADS, HD)
    selector = image[:, :, None]
    query_gain = jnp.where(selector, head_gain[1, 0][None, None, :], head_gain[0, 0][None, None, :])
    key_gain = jnp.where(selector, head_gain[1, 1][None, None, :], head_gain[0, 1][None, None, :])
    queries = head_norm(projected[:, 0], query_gain).astype(jnp.bfloat16)
    key_rows = head_norm(projected[:, 1], key_gain).astype(jnp.bfloat16)
    value_rows = projected[:, 2].astype(jnp.bfloat16)
    place = jnp.arange(TOKENS, dtype=jnp.int32)
    allowed = place[None, :] <= place[:, None]
    scale = 1.0 / math.sqrt(HD)

    def one_head(operands):
        query_head, key_head, value_head = operands
        scores = jnp.dot(query_head, key_head.T, preferred_element_type=jnp.float32) * scale
        weights = jnp.where(allowed, jnp.exp(scores), 0.0)
        totals = lax.optimization_barrier(jnp.sum(weights, axis=1, keepdims=True))
        rounded = weights.astype(jnp.bfloat16)
        weighted = jnp.dot(rounded, value_head, preferred_element_type=jnp.float32)
        return (weighted / totals).astype(jnp.bfloat16)
    per_head = lax.map(one_head, (queries.transpose(1, 0, 2), key_rows.transpose(1, 0, 2), value_rows.transpose(1, 0, 2)))
    attention = per_head.transpose(1, 0, 2).reshape(TOKENS, D)
    block = D // N_TP
    attention_blocks = attention.reshape(TOKENS, N_TP, block).transpose(1, 0, 2)
    text_blocks = output_weight[0].reshape(N_TP, block, D)
    image_blocks = output_weight[1].reshape(N_TP, block, D)

    def add_block(total, operands):
        part, text_rows, image_rows = operands
        term = jnp.where(image, jnp.dot(part, image_rows, preferred_element_type=jnp.float32), jnp.dot(part, text_rows, preferred_element_type=jnp.float32)).astype(jnp.bfloat16)
        term = lax.optimization_barrier(term)
        return (total + term.astype(jnp.float32), None)
    total, unused = lax.scan(add_block, jnp.zeros((TOKENS, D), jnp.float32), (attention_blocks, text_blocks, image_blocks))
    return total.astype(jnp.bfloat16)
```

```python
import math

import jax
import jax.numpy as jnp
from jax import lax
from jax.experimental import pallas as pl
from jax.experimental.pallas import tpu as pltpu
from jax.sharding import PartitionSpec as P

MESH = pl.DeviceIdType.MESH
F32 = jnp.float32
BF16 = jnp.bfloat16
epsilon = 1e-05
SPAN = 64
HD = 128
TOK = 512
W = 256
D = 4096
NH = 1
R = TOK // NH
H = R // 2
Q4 = H // 2
TQ = 256
QSCALE = math.log2(math.e) / math.sqrt(HD)
N_SEM = 256


def kernel(mod_ref, tok_in, gain_ref, w_in, hg_ref, w_out, out_ref,
           tok, wcat, wo, acc, ssq, qbuf, kv, o_acc, l_acc, att, term,
           r1, r2, msg, ubuf, r3, msg4, r4, fin, fin_in,
           send_sem, recv_sem, loc_sem):
    m = lax.axis_index("mod")
    z = lax.axis_index("seq")
    tp = lax.axis_index("tp")
    sib = 1 - m
    sa = 4 - 3 * m
    sb = 1 + 3 * m
    a = lax.rem(lax.div(tp, sa), 4)
    b = lax.rem(lax.div(tp, sb), 4)

    def slot(i, k):
        return lax.rem(a + i, 4) * sa + lax.rem(b + k, 4) * sb

    a_next, a_prev = {"tp": slot(1, 0)}, {"tp": slot(3, 0)}
    b_next, b_prev = {"tp": slot(0, 1)}, {"tp": slot(0, 3)}
    z_next, z_prev = {"seq": lax.rem(z + 1, 8)}, {"seq": lax.rem(z + 7, 8)}
    other = {"mod": sib}

    barrier = pltpu.get_barrier_semaphore()
    for dev in (a_next, a_prev, b_next, b_prev, z_next, z_prev, other):
        pl.semaphore_signal(barrier, inc=1, device_id=dev, device_id_type=MESH)
    pl.semaphore_wait(barrier, 7)

    sent = []
    count = [0]

    def send(src, dst, dev):
        i = count[0]
        count[0] += 1
        copy = pltpu.make_async_remote_copy(
            src_ref=src, dst_ref=dst, send_sem=send_sem.at[i], recv_sem=recv_sem.at[i],
            device_id=dev, device_id_type=MESH)
        copy.start()
        sent.append(copy)
        return copy

    def span_mod(c, block):
        s, h = divmod(c, NH)
        return mod_ref[(s * 8 + z) * TOK + h * R + block * SPAN]

    def pick(flag, one, zero):
        return jnp.where(jnp.full(one.shape, flag, jnp.int32) == 1, one, zero)

    tme = slot(0, 0)
    swap = []
    own_copies = []
    for h in range(NH):
        src = tok_in.at[pl.ds(h * R, R), :]
        dst = tok.at[m * NH + h, tme]
        swap.append(send(src, dst, other))
        cp = pltpu.make_async_copy(src, dst, loc_sem.at[h])
        cp.start()
        own_copies.append(cp)

    w_local = []
    w_remote = []
    for p in range(3):
        cp = pltpu.make_async_copy(
            w_in.at[p, :, pl.ds(pl.multiple_of(m * HD, HD), HD)],
            wcat.at[:, pl.ds(p * HD, HD)], loc_sem.at[NH + p])
        cp.start()
        w_local.append(cp)
        w_remote.append(send(
            w_in.at[p, :, pl.ds(pl.multiple_of(sib * HD, HD), HD)],
            wcat.at[:, pl.ds(384 + p * HD, HD)], other))

    def gather(c):
        rows = pl.ds(pl.multiple_of(m * H, H), H)
        low = pl.ds(pl.multiple_of(m * H, Q4), Q4)
        high = pl.ds(pl.multiple_of(m * H + Q4, Q4), Q4)

        def put(t, part, dev):
            ref = tok.at[c, t, part]
            return send(ref, ref, dev)

        acc[...] = jnp.zeros_like(acc)
        ssq[...] = jnp.zeros_like(ssq)
        own = slot(0, 0)
        ar = put(own, rows, a_next)
        al = put(own, rows, a_prev)
        bn, bp = {}, {}
        bn[0] = put(own, rows, b_next)
        bp[0] = put(own, rows, b_prev)
        yield
        d2d = {}
        ar.wait_recv()
        f1 = put(slot(3, 0), low, a_next)
        bn[3] = put(slot(3, 0), rows, b_next)
        bp[3] = put(slot(3, 0), rows, b_prev)
        d2d[3, 0] = put(slot(3, 0), rows, other)
        al.wait_recv()
        f2 = put(slot(1, 0), high, a_prev)
        bn[1] = put(slot(1, 0), rows, b_next)
        bp[1] = put(slot(1, 0), rows, b_prev)
        d2d[1, 0] = put(slot(1, 0), rows, other)
        yield
        f1.wait_recv()
        f2.wait_recv()
        bn[2] = put(slot(2, 0), rows, b_next)
        bp[2] = put(slot(2, 0), rows, b_prev)
        d2d[2, 0] = put(slot(2, 0), rows, other)
        yield
        g1, g2 = {}, {}
        for i in (0, 3, 1, 2):
            bn[i].wait_recv()
            g1[i] = put(slot(i, 3), low, b_next)
            d2d[i, 3] = put(slot(i, 3), rows, other)
            bp[i].wait_recv()
            g2[i] = put(slot(i, 1), high, b_prev)
            d2d[i, 1] = put(slot(i, 1), rows, other)
        yield
        for i in (1, 2, 3):
            d2d[i, 0].wait_recv()
        pairs(c, 3, lambda n: (n + 1, 0))
        for i in range(4):
            d2d[i, 1].wait_recv()
            d2d[i, 3].wait_recv()
        pairs(c, 8, lambda n: (lax.rem(n, 4), 1 + 2 * lax.div(n, 4)))
        for i in (0, 3, 1, 2):
            g1[i].wait_recv()
            g2[i].wait_recv()
            d2d[i, 2] = put(slot(i, 2), rows, other)
        yield
        for i in range(4):
            d2d[i, 2].wait_recv()
        pairs(c, 4, lambda n: (n, 2))
        yield

    def unit(c, t, j):
        start = pl.multiple_of(j * H, H)
        rows = pl.ds(start, H)
        x = tok[c, t, rows, :]
        first = pl.multiple_of(t * W, W)
        g = gain_ref[:, pl.ds(first, W)]
        scaled, squares = [], []
        for k in range(H // SPAN):
            flag = span_mod(c, j * (H // SPAN) + k)
            xb = x[k * SPAN:(k + 1) * SPAN].astype(F32)
            sq = xb * xb
            squares.append(sq[:, :128] + sq[:, 128:])
            scaled.append((xb * pick(flag, g[1:2], g[0:1])).astype(BF16))
        ssq[rows, :] += jnp.concatenate(squares, axis=0)
        acc[rows, :] += jnp.dot(jnp.concatenate(scaled, axis=0), wcat[pl.ds(first, W), :],
                                preferred_element_type=F32)

    def pairs(c, n, where):
        def step(q, carry):
            i, k = where(q)
            unit(c, slot(i, k), m)
            unit(c, slot(k, i), sib)
            return carry
        lax.fori_loop(0, n, step, 0)

    def own_unit(c):
        def step(j, carry):
            unit(c, slot(0, 0), j)
            return carry
        lax.fori_loop(0, 2, step, 0)

    def finish_qkv(c):
        def step(k, carry):
            r0 = pl.multiple_of(k * SPAN, SPAN)
            flag = span_mod(c, k)
            mine = (jnp.full((SPAN, 3 * HD), flag, jnp.int32) == m)
            block = acc[pl.ds(r0, SPAN), :]
            block = jnp.where(mine, block[:, :3 * HD], block[:, 3 * HD:])
            mean = jnp.sum(ssq[pl.ds(r0, SPAN), :], axis=1, keepdims=True) * (1.0 / D)
            block = block * lax.rsqrt(mean + epsilon)
            qp, kp, vp = block[:, :HD], block[:, HD:2 * HD], block[:, 2 * HD:]
            qg = pick(flag, hg_ref[1, 0:1], hg_ref[0, 0:1])
            kg = pick(flag, hg_ref[1, 1:2], hg_ref[0, 1:2])
            qm = jnp.mean(qp * qp, axis=1, keepdims=True)
            km = jnp.mean(kp * kp, axis=1, keepdims=True)
            qbuf[pl.ds(c * R + r0, SPAN), :] = (qp * lax.rsqrt(qm + epsilon) * (qg * QSCALE)).astype(BF16)
            kv[c, z, pl.ds(r0, SPAN), 0:HD] = (kp * lax.rsqrt(km + epsilon) * kg).astype(BF16)
            kv[c, z, pl.ds(r0, SPAN), HD:2 * HD] = vp.astype(BF16)
            return carry
        lax.fori_loop(0, R // SPAN, step, 0)

    low_half = pl.ds(0, R // 2)
    high_half = pl.ds(R // 2, R // 2)

    def zring(c):
        def put(src_z, part, dev):
            ref = kv.at[c, lax.rem(src_z, 8), part]
            return send(ref, ref, dev)
        full = pl.ds(0, R)
        right = put(z, full, z_next)
        left = put(z, full, z_prev)
        yield
        for d in (1, 2, 3):
            right.wait_recv()
            right = put(z + 8 - d, full if d < 3 else low_half, z_next)
            left.wait_recv()
            left = put(z + d, full if d < 3 else high_half, z_prev)
            yield
        right.wait_recv()
        left.wait_recv()
        yield

    def tile(c, src, r0, diagonal):
        rows = pl.ds(r0, TQ)
        s = lax.dot_general(qbuf[rows, :], kv[c, src, :, 0:HD], (((1,), (1,)), ((), ())),
                            preferred_element_type=F32)
        p = jnp.exp2(s)
        if diagonal:
            at = lax.broadcasted_iota(jnp.int32, p.shape, 0) + (r0 - c * R)
            p = jnp.where(lax.broadcasted_iota(jnp.int32, p.shape, 1) <= at, p, 0.0)
        total = p[:, 0:128]
        for k in range(1, R // 128):
            total = total + p[:, k * 128:(k + 1) * 128]
        l_acc[rows, :] += total
        o_acc[rows, :] += jnp.dot(p.astype(BF16), kv[c, src, :, HD:2 * HD], preferred_element_type=F32)

    def attend(c, src, lo, hi, diagonal=False):
        def step(n, carry):
            tile(c, src, pl.multiple_of(n * TQ, TQ), diagonal)
            return carry
        lax.fori_loop(lo, hi, step, 0)

    half = TOK // TQ

    def attend_own(c):
        first = c * R // TQ
        attend(c, z, first, first + R // TQ, True)
        if first + R // TQ < 2 * half:
            attend(c, z, first + R // TQ, 2 * half)

    def attend_from(c, src):
        if c < NH:
            attend(c, src, jnp.where(src < z, 0, half), 2 * half)
        else:
            attend(c, src, jnp.where(src < z, half, 2 * half), 2 * half)

    def attend_step(c, d):
        attend_from(c, lax.rem(z + 8 - d, 8))
        if d < 4:
            attend_from(c, lax.rem(z + d, 8))

    def reduce(c):
        rows = pl.ds(c * R, R)
        total = jnp.sum(l_acc[rows, :], axis=1, keepdims=True)
        att[c, m] = (o_acc[rows, :] / total).astype(BF16)
        ref = att.at[c, m]
        swapped = send(ref, ref, other)
        yield
        swapped.wait_recv()

        def product(g):
            def step(k, carry):
                r0 = pl.multiple_of(k * 128, 128)
                left, right = [], []
                for n in range(2):
                    flag = span_mod(c, k * 2 + n)
                    mine = (jnp.full((SPAN, HD), flag, jnp.int32) == m)
                    parts = [att[c, h, pl.ds(r0 + n * SPAN, SPAN), :] for h in range(2)]
                    zero = jnp.zeros((SPAN, HD), BF16)
                    left.append(jnp.concatenate([jnp.where(mine, q, zero) for q in parts], axis=1))
                    right.append(jnp.concatenate([jnp.where(mine, zero, q) for q in parts], axis=1))
                lhs = jnp.concatenate(
                    [jnp.concatenate(left, axis=0), jnp.concatenate(right, axis=0)], axis=1)
                res = jnp.dot(lhs, wo[lax.rem(a + g, 4)], preferred_element_type=F32).astype(BF16)
                for k4 in range(4):
                    term[c, g, k4, pl.ds(r0, 128), :] = res[:, k4 * 128:(k4 + 1) * 128]
                return carry
            lax.fori_loop(0, R // 128, step, 0)

        product(2)
        s1 = send(term.at[c, 2, :, low_half], r1.at[c, 0], a_next)
        s2 = send(term.at[c, 2, :, high_half], r1.at[c, 1], a_prev)

        def rest(n, carry):
            product(jnp.where(n == 2, 0, 2 * n + 1))
            return carry
        lax.fori_loop(0, 3, rest, 0)
        yield

        def add(x, y):
            return (x.astype(F32) + y.astype(F32)).astype(BF16)

        s1.wait_recv()
        msg[c, 0, :, low_half] = add(term[c, 1, :, low_half], r1[c, 0])
        msg[c, 0, :, high_half] = term[c, 1, :, high_half]
        s3 = send(msg.at[c, 0], r2.at[c, 0], a_next)
        s2.wait_recv()
        msg[c, 1, :, high_half] = add(term[c, 3, :, high_half], r1[c, 1])
        msg[c, 1, :, low_half] = term[c, 3, :, low_half]
        s4 = send(msg.at[c, 1], r2.at[c, 1], a_prev)
        yield
        s3.wait_recv()
        s4.wait_recv()

        def total4(k, carry):
            ubuf[c, k] = (term[c, 0, k].astype(F32) + r2[c, 0, k].astype(F32)
                          + r2[c, 1, k].astype(F32)).astype(BF16)
            return carry

        total4(lax.rem(b + 2, 4), 0)
        s5 = send(ubuf.at[c, lax.rem(b + 2, 4), low_half], r3.at[c, 0], b_next)
        s6 = send(ubuf.at[c, lax.rem(b + 2, 4), high_half], r3.at[c, 1], b_prev)
        total4(lax.rem(b + 1, 4), 0)
        total4(lax.rem(b + 3, 4), 0)
        total4(b, 0)
        yield
        s5.wait_recv()
        up, down = lax.rem(b + 1, 4), lax.rem(b + 3, 4)
        msg4[c, 0, low_half] = add(ubuf[c, up, low_half], r3[c, 0])
        msg4[c, 0, high_half] = ubuf[c, up, high_half]
        s7 = send(msg4.at[c, 0], r4.at[c, 0], b_next)
        s6.wait_recv()
        msg4[c, 1, high_half] = add(ubuf[c, down, high_half], r3[c, 1])
        msg4[c, 1, low_half] = ubuf[c, down, low_half]
        s8 = send(msg4.at[c, 1], r4.at[c, 1], b_prev)
        yield
        s7.wait_recv()
        s8.wait_recv()
        fin[c] = (ubuf[c, b].astype(F32) + r4[c, 0].astype(F32) + r4[c, 1].astype(F32)).astype(BF16)
        yield

    def go(stream, n=1):
        for _ in range(n):
            next(stream)

    for cp in own_copies:
        cp.wait()
    for cp in swap:
        cp.wait_recv()
    gathers = [gather(c) for c in range(2 * NH)]
    rings = [zring(c) for c in range(2 * NH)]
    sums = [reduce(c) for c in range(2 * NH)]

    go(gathers[0], 1)
    wo_local = []
    for i in range(4):
        for k in range(4):
            t = i * sa + k * sb
            cp = pltpu.make_async_copy(
                w_out.at[:, pl.ds(pl.multiple_of(t * W + m * HD, HD), HD)],
                wo.at[i, pl.ds(0, 256), pl.ds(k * HD, HD)], loc_sem.at[NH + 3 + i * 4 + k])
            cp.start()
            wo_local.append(cp)
    wo_remote = []
    o_acc[...] = jnp.zeros_like(o_acc)
    l_acc[...] = jnp.zeros_like(l_acc)
    go(gathers[0], 2)
    for cp in w_local:
        cp.wait()
    for cp in w_remote:
        cp.wait_recv()
    own_unit(0)
    go(gathers[0], 3)
    for i in range(4):
        for k in range(4):
            t = i * sb + k * sa
            wo_remote.append(send(
                w_out.at[:, pl.ds(pl.multiple_of(t * W + sib * HD, HD), HD)],
                wo.at[i, pl.ds(256, 256), pl.ds(k * HD, HD)], other))
    finish_qkv(0)
    go(rings[0])
    go(gathers[1])
    own_unit(1)
    go(gathers[1], 2)
    go(rings[0])
    go(gathers[1], 1)
    go(gathers[1], 2)
    finish_qkv(1)
    go(rings[1])
    go(rings[0])
    attend_own(0)
    attend_step(0, 1)
    go(rings[0])
    attend_step(0, 2)
    attend_own(1)
    go(rings[0])
    go(rings[1])
    attend_step(0, 3)
    attend_step(0, 4)
    for cp in wo_local:
        cp.wait()
    for cp in wo_remote:
        cp.wait_recv()
    go(sums[0])
    attend_step(1, 1)
    go(sums[0])
    go(rings[1])
    go(sums[0])
    attend_step(1, 2)
    go(rings[1])
    go(sums[0])
    attend_step(1, 3)
    go(sums[0])
    go(rings[1])
    attend_step(1, 4)
    go(sums[1], 1)
    go(sums[0], 1)
    go(sums[1], 5)

    back = []
    for h in range(NH):
        back.append(send(fin.at[sib * NH + h], fin_in.at[h], other))
    for h in range(NH):
        back[h].wait_recv()
        own = fin[m * NH + h]
        got = fin_in[h]
        lower = jnp.full(own.shape, m, jnp.int32) == 0
        out_ref[h * R:(h + 1) * R, 0:HD] = jnp.where(lower, own, got)
        out_ref[h * R:(h + 1) * R, HD:2 * HD] = jnp.where(lower, got, own)
    for cp in sent:
        cp.wait_send()


def body(tokens, modality, norm_gain, input_weight, head_gain, output_weight):
    chunks = 2 * NH
    vmem = pl.BlockSpec(memory_space=pltpu.VMEM)
    anywhere = pl.BlockSpec(memory_space=pl.ANY)
    w3 = jnp.transpose(input_weight[0], (1, 0, 2))
    return pl.pallas_call(
        kernel,
        out_shape=jax.ShapeDtypeStruct((TOK, W), BF16),
        in_specs=[pl.BlockSpec(memory_space=pltpu.SMEM), vmem, vmem, anywhere, vmem, anywhere],
        out_specs=vmem,
        scratch_shapes=[
            pltpu.VMEM((chunks, 16, R, W), BF16),
            pltpu.VMEM((D, 6 * HD), BF16),
            pltpu.VMEM((4, 512, 512), BF16),
            pltpu.VMEM((R, 6 * HD), F32),
            pltpu.VMEM((R, 128), F32),
            pltpu.VMEM((2 * TOK, HD), BF16),
            pltpu.VMEM((chunks, 8, R, 2 * HD), BF16),
            pltpu.VMEM((2 * TOK, HD), F32),
            pltpu.VMEM((2 * TOK, 128), F32),
            pltpu.VMEM((chunks, 2, R, HD), BF16),
            pltpu.VMEM((chunks, 4, 4, R, 128), BF16),
            pltpu.VMEM((chunks, 2, 4, R // 2, 128), BF16),
            pltpu.VMEM((chunks, 2, 4, R, 128), BF16),
            pltpu.VMEM((chunks, 2, 4, R, 128), BF16),
            pltpu.VMEM((chunks, 4, R, 128), BF16),
            pltpu.VMEM((chunks, 2, R // 2, 128), BF16),
            pltpu.VMEM((chunks, 2, R, 128), BF16),
            pltpu.VMEM((chunks, 2, R, 128), BF16),
            pltpu.VMEM((chunks, R, 128), BF16),
            pltpu.VMEM((NH, R, 128), BF16),
            pltpu.SemaphoreType.DMA((N_SEM,)),
            pltpu.SemaphoreType.DMA((N_SEM,)),
            pltpu.SemaphoreType.DMA((NH + 3 + 16,)),
        ],
        compiler_params=pltpu.CompilerParams(
            collective_id=0, has_side_effects=True, vmem_limit_bytes=56 * 1024 * 1024),
    )(modality, tokens, norm_gain, w3, head_gain, output_weight[0])


def solution(mesh):
    in_specs = (
        P(("mod", "seq"), "tp"),
        P(),
        P(),
        P("mod", None, None, "tp"),
        P(),
        P("mod", "tp", None),
    )
    out_specs = P(("mod", "seq"), "tp")
    return jax.shard_map(body, mesh=mesh, in_specs=in_specs, out_specs=out_specs, check_vma=False)
```

```python
import math

import jax
import jax.numpy as jnp
from jax import lax
from jax.experimental import pallas as pl
from jax.experimental.pallas import tpu as pltpu
from jax.sharding import PartitionSpec as P

MESH = pl.DeviceIdType.MESH
F32 = jnp.float32
BF16 = jnp.bfloat16
epsilon = 1e-05
SPAN = 64
HD = 128
TOK = 512
W = 256
D = 4096
NH = 2
R = TOK // NH
H = R // 2
Q4 = H // 2
TQ = 256
ORDER = (
    "G0", "G0", "G0", "Q0", "Q1", "Q2", "Q3", "G0", "G0", "G0", "G1", "G0", "Q0", "G0", "Q0", "G0",
    "G0", "G1", "G1", "G0", "G0", "Q0", "G1", "G1", "G1", "G2", "G1", "Q0", "Q0", "Z0", "Q1", "Q1",
    "G1", "G1", "G1", "G2", "G2", "G1", "G1", "Z0", "Z0", "Q1", "G2", "G2", "G2", "G2", "G3", "Q1",
    "Q1", "Z1", "Q2", "Q2", "Z0", "Z0", "G2", "G2", "G2", "G2", "ALL0", "G3", "G3", "G2", "Z1", "Z1",
    "ALL1", "Q2", "G3", "G3", "G3", "G3", "Q2", "Z0", "Z0", "Q2", "Z2", "Q3", "Q3", "Z1", "Z1", "G3",
    "G3", "G3", "G3", "ALL2", "G3", "Q3", "Z2", "Z2", "Q3", "Q3", "Z3", "AUU0", "Z1", "Z1", "ALL3", "ALU0",
    "ALU1", "Z2", "Z2", "ALU2", "ALU3", "Z3", "Z3", "AUU1", "ALL4", "R0", "R1", "ALU4", "R0", "R0", "Z2", "Z2",
    "R1", "R1", "Z3", "Z3", "AUU2", "R0", "R0", "R1", "R1", "Z3", "Z3", "AUU3", "R0", "R0", "AUU4", "R2",
    "R3", "R0", "R1", "R0", "R1", "R2", "R2", "R3", "R3", "R0", "R1", "R1", "R2", "R2", "R3", "R3",
    "R1", "R2", "R2", "R3", "R2", "R3", "R2", "R3", "R3", "R2", "R3",
)
QSCALE = math.log2(math.e) / math.sqrt(HD)
N_SEM = 256


def kernel(mod_ref, tok_in, gain_ref, w_in, hg_ref, w_out, out_ref,
           tok, wcat, wo, acc, ssq, qbuf, kv, o_acc, l_acc, att, term,
           abuf, r1, r2, msg, ubuf, r3, msg4, r4, fin, fin_in,
           send_sem, recv_sem, loc_sem):
    m = lax.axis_index("mod")
    z = lax.axis_index("seq")
    tp = lax.axis_index("tp")
    sib = 1 - m
    sa = 4 - 3 * m
    sb = 1 + 3 * m
    a = lax.rem(lax.div(tp, sa), 4)
    b = lax.rem(lax.div(tp, sb), 4)

    def slot(i, k):
        return lax.rem(a + i, 4) * sa + lax.rem(b + k, 4) * sb

    a_next, a_prev = {"tp": slot(1, 0)}, {"tp": slot(3, 0)}
    b_next, b_prev = {"tp": slot(0, 1)}, {"tp": slot(0, 3)}
    z_next, z_prev = {"seq": lax.rem(z + 1, 8)}, {"seq": lax.rem(z + 7, 8)}
    other = {"mod": sib}

    barrier = pltpu.get_barrier_semaphore()
    for dev in (a_next, a_prev, b_next, b_prev, z_next, z_prev, other):
        pl.semaphore_signal(barrier, inc=1, device_id=dev, device_id_type=MESH)
    pl.semaphore_wait(barrier, 7)

    sent = []
    count = [0]

    def send(src, dst, dev):
        i = count[0]
        count[0] += 1
        copy = pltpu.make_async_remote_copy(
            src_ref=src, dst_ref=dst, send_sem=send_sem.at[i], recv_sem=recv_sem.at[i],
            device_id=dev, device_id_type=MESH)
        copy.start()
        sent.append(copy)
        return copy

    landed = set()

    def arrive(*copies):
        for copy in copies:
            if id(copy) not in landed:
                landed.add(id(copy))
                copy.wait_recv()

    def span_mod(c, block):
        s, h = divmod(c, NH)
        return mod_ref[(s * 8 + z) * TOK + h * R + block * SPAN]

    def pick(flag, one, zero):
        return jnp.where(jnp.full(one.shape, flag, jnp.int32) == 1, one, zero)

    tme = slot(0, 0)
    swap = []
    own_copies = []
    for h in range(NH):
        src = tok_in.at[pl.ds(h * R, R), :]
        dst = tok.at[m * NH + h, tme]
        swap.append(send(src, dst, other))
        cp = pltpu.make_async_copy(src, dst, loc_sem.at[h])
        cp.start()
        own_copies.append(cp)

    w_local = []
    w_remote = []
    for p in range(3):
        cp = pltpu.make_async_copy(
            w_in.at[p, :, pl.ds(pl.multiple_of(m * HD, HD), HD)],
            wcat.at[:, pl.ds(p * HD, HD)], loc_sem.at[NH + p])
        cp.start()
        w_local.append(cp)
        w_remote.append(send(
            w_in.at[p, :, pl.ds(pl.multiple_of(sib * HD, HD), HD)],
            wcat.at[:, pl.ds(384 + p * HD, HD)], other))

    hops = {}

    def gather(c):
        rows = pl.ds(pl.multiple_of(m * H, H), H)
        low = pl.ds(pl.multiple_of(m * H, Q4), Q4)
        high = pl.ds(pl.multiple_of(m * H + Q4, Q4), Q4)

        def put(t, part, dev):
            ref = tok.at[c, t, part]
            return send(ref, ref, dev)

        own = slot(0, 0)
        ar = put(own, rows, a_next)
        al = put(own, rows, a_prev)
        bn, bp = {}, {}
        d2d = hops[c] = {}
        bn[0] = put(own, rows, b_next)
        bp[0] = put(own, rows, b_prev)
        yield
        arrive(ar)
        f1 = put(slot(3, 0), low, a_next)
        bn[3] = put(slot(3, 0), rows, b_next)
        bp[3] = put(slot(3, 0), rows, b_prev)
        d2d[3, 0] = put(slot(3, 0), rows, other)
        yield
        arrive(al)
        f2 = put(slot(1, 0), high, a_prev)
        bn[1] = put(slot(1, 0), rows, b_next)
        bp[1] = put(slot(1, 0), rows, b_prev)
        d2d[1, 0] = put(slot(1, 0), rows, other)
        yield
        arrive(f1, f2)
        bn[2] = put(slot(2, 0), rows, b_next)
        bp[2] = put(slot(2, 0), rows, b_prev)
        d2d[2, 0] = put(slot(2, 0), rows, other)
        yield
        g1, g2 = {}, {}
        for i in (0, 3, 1, 2):
            arrive(bn[i])
            g1[i] = put(slot(i, 3), low, b_next)
            d2d[i, 3] = put(slot(i, 3), rows, other)
            arrive(bp[i])
            g2[i] = put(slot(i, 1), high, b_prev)
            d2d[i, 1] = put(slot(i, 1), rows, other)
            yield
        for i in (0, 3, 1, 2):
            arrive(g1[i], g2[i])
            d2d[i, 2] = put(slot(i, 2), rows, other)
            yield

    def unit(c, t):
        x = tok[c, t]
        first = pl.multiple_of(t * W, W)
        g = gain_ref[:, pl.ds(first, W)]
        scaled, squares = [], []
        for k in range(R // SPAN):
            flag = span_mod(c, k)
            xb = x[k * SPAN:(k + 1) * SPAN].astype(F32)
            sq = xb * xb
            squares.append(sq[:, :128] + sq[:, 128:])
            scaled.append((xb * pick(flag, g[1:2], g[0:1])).astype(BF16))
        return (jnp.concatenate(squares, axis=0),
                jnp.dot(jnp.concatenate(scaled, axis=0), wcat[pl.ds(first, W), :],
                        preferred_element_type=F32))

    def units(c, n, where):
        def step(q, carry):
            i, k = where(q)
            squares, part = unit(c, slot(i, k))
            ssq[c] += squares
            acc[c] += part
            return carry
        lax.fori_loop(0, n, step, 0)

    def project(c):
        ssq[c], acc[c] = unit(c, slot(0, 0))
        yield
        d2d = hops[c]
        near = [(i, k) for i in (0, 1, 3) for k in (0, 1, 3) if (i, k) != (0, 0)]

        def grid9(q):
            i, k = lax.div(q, 3), lax.rem(q, 3)
            return i + lax.div(i, 2), k + lax.div(k, 2)

        arrive(*[d2d[p] for p in near])
        units(c, 4, lambda q: grid9(q + 1))
        yield
        units(c, 4, lambda q: grid9(q + 5))
        yield
        arrive(*[d2d[i, k] for i in range(4) for k in range(4) if 2 in (i, k)])
        units(c, 4, lambda q: (2, q))
        yield
        units(c, 3, lambda q: (q + lax.div(q, 2), 2))
        yield
        finish_qkv(c)
        yield

    def finish_qkv(c):
        def step(k, carry):
            r0 = pl.multiple_of(k * SPAN, SPAN)
            flag = span_mod(c, k)
            mine = (jnp.full((SPAN, 3 * HD), flag, jnp.int32) == m)
            block = acc[c, pl.ds(r0, SPAN), :]
            block = jnp.where(mine, block[:, :3 * HD], block[:, 3 * HD:])
            mean = jnp.sum(ssq[c, pl.ds(r0, SPAN), :], axis=1, keepdims=True) * (1.0 / D)
            block = block * lax.rsqrt(mean + epsilon)
            qp, kp, vp = block[:, :HD], block[:, HD:2 * HD], block[:, 2 * HD:]
            qg = pick(flag, hg_ref[1, 0:1], hg_ref[0, 0:1])
            kg = pick(flag, hg_ref[1, 1:2], hg_ref[0, 1:2])
            qm = jnp.mean(qp * qp, axis=1, keepdims=True)
            km = jnp.mean(kp * kp, axis=1, keepdims=True)
            qbuf[pl.ds(c * R + r0, SPAN), :] = (qp * lax.rsqrt(qm + epsilon) * (qg * QSCALE)).astype(BF16)
            kv[c // NH, z, pl.ds(c % NH * R + r0, SPAN), 0:HD] = (kp * lax.rsqrt(km + epsilon) * kg).astype(BF16)
            kv[c // NH, z, pl.ds(c % NH * R + r0, SPAN), HD:2 * HD] = vp.astype(BF16)
            return carry
        lax.fori_loop(0, R // SPAN, step, 0)

    ring = {}

    def zring(c):
        def put(src_z, first, count, dev):
            ref = kv.at[c // NH, lax.rem(src_z, 8), pl.ds(c % NH * R + first, count)]
            return send(ref, ref, dev)

        ring[c, "r", 1] = put(z, 0, R, z_next)
        ring[c, "l", 1] = put(z, 0, R, z_prev)
        yield
        for d in (1, 2, 3):
            count = R if d < 3 else R // 2
            arrive(ring[c, "r", d])
            ring[c, "r", d + 1] = put(z + 8 - d, 0, count, z_next)
            yield
            arrive(ring[c, "l", d])
            ring[c, "l", d + 1] = put(z + d, R - count, count, z_prev)
            yield

    def tile(shard, src, r0, diagonal):
        rows = pl.ds(r0, TQ)
        s = lax.dot_general(qbuf[rows, :], kv[shard, src, :, 0:HD], (((1,), (1,)), ((), ())),
                            preferred_element_type=F32)
        p = jnp.exp2(s)
        if diagonal:
            at = lax.broadcasted_iota(jnp.int32, p.shape, 0) + (r0 - shard * TOK)
            p = jnp.where(lax.broadcasted_iota(jnp.int32, p.shape, 1) <= at, p, 0.0)
        total = p[:, 0:128]
        for k in range(1, TOK // 128):
            total = total + p[:, k * 128:(k + 1) * 128]
        l_acc[rows, :] += total
        o_acc[rows, :] += jnp.dot(p.astype(BF16), kv[shard, src, :, HD:2 * HD], preferred_element_type=F32)

    half = TOK // TQ

    def attend(shard, target, d):
        first = target * half
        if d == 0:
            def own(n, carry):
                tile(shard, z, pl.multiple_of(n * TQ, TQ), shard == target)
                return carry
            lax.fori_loop(first, first + half, own, 0)
            return
        for h in range(NH):
            arrive(ring[shard * NH + h, "r", d], ring[shard * NH + h, "l", d])

        def side(q, carry):
            src = lax.rem(z + 8 - d + q * 2 * d, 8)

            def step(n, inner):
                tile(shard, src, pl.multiple_of(n * TQ, TQ), False)
                return inner
            seen = first + half if shard < target else jnp.where(src < z, first + half, first)
            lax.fori_loop(first, seen, step, 0)
            return carry
        lax.fori_loop(0, 2 if d < 4 else 1, side, 0)

    low_half = pl.ds(0, R // 2)
    high_half = pl.ds(R // 2, R // 2)

    def reduce(c):
        rows = pl.ds(c * R, R)
        total = jnp.sum(l_acc[rows, :], axis=1, keepdims=True)
        att[c, m] = (o_acc[rows, :] / total).astype(BF16)
        ref = att.at[c, m]
        swapped = send(ref, ref, other)
        yield
        arrive(swapped)

        zero = jnp.zeros((SPAN, HD), BF16)
        for n in range(R // SPAN):
            mine = (jnp.full((SPAN, HD), span_mod(c, n), jnp.int32) == m)
            for h in range(2):
                part = att[c, h, n * SPAN:(n + 1) * SPAN, :]
                abuf[c, n * SPAN:(n + 1) * SPAN, h * HD:(h + 1) * HD] = jnp.where(mine, part, zero)
                abuf[c, n * SPAN:(n + 1) * SPAN, 256 + h * HD:256 + (h + 1) * HD] = jnp.where(mine, zero, part)

        def product(g):
            res = jnp.dot(abuf[c], wo[lax.rem(a + g, 4)], preferred_element_type=F32).astype(BF16)
            for k4 in range(4):
                term[c, g, k4] = res[:, k4 * 128:(k4 + 1) * 128]

        product(2)
        s1 = send(term.at[c, 2, :, low_half], r1.at[c, 0], a_next)
        s2 = send(term.at[c, 2, :, high_half], r1.at[c, 1], a_prev)
        yield

        def rest(n, carry):
            product(jnp.where(n == 2, 0, 2 * n + 1))
            return carry
        lax.fori_loop(0, 3, rest, 0)
        yield

        def add(x, y):
            return (x.astype(F32) + y.astype(F32)).astype(BF16)

        arrive(s1)
        msg[c, 0, :, low_half] = add(term[c, 1, :, low_half], r1[c, 0])
        msg[c, 0, :, high_half] = term[c, 1, :, high_half]
        s3 = send(msg.at[c, 0], r2.at[c, 0], a_next)
        yield
        arrive(s2)
        msg[c, 1, :, high_half] = add(term[c, 3, :, high_half], r1[c, 1])
        msg[c, 1, :, low_half] = term[c, 3, :, low_half]
        s4 = send(msg.at[c, 1], r2.at[c, 1], a_prev)
        yield
        arrive(s3, s4)

        def total4(k, carry):
            ubuf[c, k] = (term[c, 0, k].astype(F32) + r2[c, 0, k].astype(F32)
                          + r2[c, 1, k].astype(F32)).astype(BF16)
            return carry

        total4(lax.rem(b + 2, 4), 0)
        s5 = send(ubuf.at[c, lax.rem(b + 2, 4), low_half], r3.at[c, 0], b_next)
        s6 = send(ubuf.at[c, lax.rem(b + 2, 4), high_half], r3.at[c, 1], b_prev)
        yield
        total4(lax.rem(b + 1, 4), 0)
        total4(lax.rem(b + 3, 4), 0)
        total4(b, 0)
        yield
        arrive(s5)
        up, down = lax.rem(b + 1, 4), lax.rem(b + 3, 4)
        msg4[c, 0, low_half] = add(ubuf[c, up, low_half], r3[c, 0])
        msg4[c, 0, high_half] = ubuf[c, up, high_half]
        s7 = send(msg4.at[c, 0], r4.at[c, 0], b_next)
        yield
        arrive(s6)
        msg4[c, 1, high_half] = add(ubuf[c, down, high_half], r3[c, 1])
        msg4[c, 1, low_half] = ubuf[c, down, low_half]
        s8 = send(msg4.at[c, 1], r4.at[c, 1], b_prev)
        yield
        arrive(s7, s8)
        fin[c] = (ubuf[c, b].astype(F32) + r4[c, 0].astype(F32) + r4[c, 1].astype(F32)).astype(BF16)
        yield

    streams = {}
    for c in range(2 * NH):
        streams["G%d" % c] = gather(c)
        streams["Q%d" % c] = project(c)
        streams["Z%d" % c] = zring(c)
        streams["R%d" % c] = reduce(c)

    wo_local, wo_remote = [], []
    for i in range(4):
        for k in range(4):
            t = i * sa + k * sb
            cp = pltpu.make_async_copy(
                w_out.at[:, pl.ds(pl.multiple_of(t * W + m * HD, HD), HD)],
                wo.at[i, pl.ds(0, 256), pl.ds(k * HD, HD)], loc_sem.at[NH + 3 + i * 4 + k])
            cp.start()
            wo_local.append(cp)
    for cp in own_copies:
        cp.wait()
    arrive(*swap)
    seen = set()
    for name in ORDER:
        if name[0] == "A":
            attend("LU".index(name[1]), "LU".index(name[2]), int(name[3]))
            continue
        if name[0] == "Q" and "Q" not in seen:
            seen.add("Q")
            o_acc[...] = jnp.zeros_like(o_acc)
            l_acc[...] = jnp.zeros_like(l_acc)
            for cp in w_local:
                cp.wait()
            arrive(*w_remote)
        if name == "Z0" and "Z" not in seen:
            seen.add("Z")
            for i in range(4):
                for k in range(4):
                    t = i * sb + k * sa
                    wo_remote.append(send(
                        w_out.at[:, pl.ds(pl.multiple_of(t * W + sib * HD, HD), HD)],
                        wo.at[i, pl.ds(256, 256), pl.ds(k * HD, HD)], other))
        if name[0] == "R" and "R" not in seen:
            seen.add("R")
            for cp in wo_local:
                cp.wait()
            arrive(*wo_remote)
        next(streams[name])

    back = []
    for h in range(NH):
        back.append(send(fin.at[sib * NH + h], fin_in.at[h], other))
    for h in range(NH):
        arrive(back[h])
        own = fin[m * NH + h]
        got = fin_in[h]
        lower = jnp.full(own.shape, m, jnp.int32) == 0
        out_ref[h * R:(h + 1) * R, 0:HD] = jnp.where(lower, own, got)
        out_ref[h * R:(h + 1) * R, HD:2 * HD] = jnp.where(lower, got, own)
    for cp in sent:
        cp.wait_send()


def body(tokens, modality, norm_gain, input_weight, head_gain, output_weight):
    chunks = 2 * NH
    vmem = pl.BlockSpec(memory_space=pltpu.VMEM)
    anywhere = pl.BlockSpec(memory_space=pl.ANY)
    w3 = jnp.transpose(input_weight[0], (1, 0, 2))
    return pl.pallas_call(
        kernel,
        out_shape=jax.ShapeDtypeStruct((TOK, W), BF16),
        in_specs=[pl.BlockSpec(memory_space=pltpu.SMEM), vmem, vmem, anywhere, vmem, anywhere],
        out_specs=vmem,
        scratch_shapes=[
            pltpu.VMEM((chunks, 16, R, W), BF16),
            pltpu.VMEM((D, 6 * HD), BF16),
            pltpu.VMEM((4, 512, 512), BF16),
            pltpu.VMEM((chunks, R, 6 * HD), F32),
            pltpu.VMEM((chunks, R, 128), F32),
            pltpu.VMEM((2 * TOK, HD), BF16),
            pltpu.VMEM((2, 8, TOK, 2 * HD), BF16),
            pltpu.VMEM((2 * TOK, HD), F32),
            pltpu.VMEM((2 * TOK, 128), F32),
            pltpu.VMEM((chunks, 2, R, HD), BF16),
            pltpu.VMEM((chunks, 4, 4, R, 128), BF16),
            pltpu.VMEM((chunks, R, 512), BF16),
            pltpu.VMEM((chunks, 2, 4, R // 2, 128), BF16),
            pltpu.VMEM((chunks, 2, 4, R, 128), BF16),
            pltpu.VMEM((chunks, 2, 4, R, 128), BF16),
            pltpu.VMEM((chunks, 4, R, 128), BF16),
            pltpu.VMEM((chunks, 2, R // 2, 128), BF16),
            pltpu.VMEM((chunks, 2, R, 128), BF16),
            pltpu.VMEM((chunks, 2, R, 128), BF16),
            pltpu.VMEM((chunks, R, 128), BF16),
            pltpu.VMEM((NH, R, 128), BF16),
            pltpu.SemaphoreType.DMA((N_SEM,)),
            pltpu.SemaphoreType.DMA((N_SEM,)),
            pltpu.SemaphoreType.DMA((NH + 3 + 16,)),
        ],
        compiler_params=pltpu.CompilerParams(
            collective_id=0, has_side_effects=True, vmem_limit_bytes=56 * 1024 * 1024),
    )(modality, tokens, norm_gain, w3, head_gain, output_weight[0])


def solution(mesh):
    in_specs = (
        P(("mod", "seq"), "tp"),
        P(),
        P(),
        P("mod", None, None, "tp"),
        P(),
        P("mod", "tp", None),
    )
    out_specs = P(("mod", "seq"), "tp")
    return jax.shard_map(body, mesh=mesh, in_specs=in_specs, out_specs=out_specs, check_vma=False)
```

```python
import math

import jax
import jax.numpy as jnp
from jax import lax
from jax.experimental import pallas as pl
from jax.experimental.pallas import tpu as pltpu
from jax.sharding import PartitionSpec as P

MESH = pl.DeviceIdType.MESH
F32 = jnp.float32
BF16 = jnp.bfloat16
epsilon = 1e-05
SPAN = 64
HD = 128
TOK = 512
W = 256
D = 4096
NH = 2
R = TOK // NH
H = R // 2
Q4 = H // 2
TQ = 256
ORDER = (
    "G0", "G0", "G0", "Q0", "G0", "G0", "G1", "Q3", "Q1", "Q2", "G0", "G0", "G0", "G0", "Q0", "G1",
    "G1", "Q0", "G0", "G1", "G0", "G1", "G0", "Q0", "G1", "G1", "Q0", "G1", "G1", "G2", "Q0", "Z0",
    "Q1", "G1", "Q1", "G1", "G1", "G2", "G2", "G3", "Q1", "Z0", "Z0", "G2", "G2", "Q1", "Q1", "Z1",
    "G2", "ALL0", "G2", "G3", "G3", "Q2", "Z0", "Z0", "G3", "G3", "G2", "G2", "Q2", "G3", "G2", "G2",
    "Z1", "Z1", "G3", "ALL1", "G3", "G3", "Q3", "Z0", "Z0", "G3", "G2", "G3", "Q3", "Q2", "Z1", "Z1",
    "G3", "Q2", "Q2", "Z2", "Q3", "Q3", "Q3", "Z3", "AUU0", "Z1", "Z1", "ALL3", "ALL2", "ALU0", "Z2", "Z2",
    "ALU2", "ALU1", "Z3", "Z3", "AUU1", "ALL4", "R0", "R1", "ALU4", "ALU3", "Z2", "Z2", "R0", "R0", "R1", "R1",
    "Z3", "Z3", "AUU2", "R0", "R0", "Z2", "Z2", "R1", "R1", "Z3", "Z3", "AUU3", "R0", "AUU4", "R2", "R3",
    "R2", "R1", "R2", "R3", "R0", "R3", "R2", "R2", "R1", "R3", "R3", "R2", "R3", "R2", "R3",
)
QSCALE = math.log2(math.e) / math.sqrt(HD)
N_SEM = 256


def kernel(mod_ref, tok_in, gain_ref, w_in, hg_ref, w_out, out_ref,
           tok, wcat, wo, acc, ssq, qbuf, kv, o_acc, l_acc, att, term,
           abuf, r1, r2, msg, ubuf, r4, fin, fin_in,
           send_sem, recv_sem, loc_sem):
    m = lax.axis_index("mod")
    z = lax.axis_index("seq")
    tp = lax.axis_index("tp")
    sib = 1 - m
    sa = 4 - 3 * m
    sb = 1 + 3 * m
    a = lax.rem(lax.div(tp, sa), 4)
    b = lax.rem(lax.div(tp, sb), 4)

    def slot(i, k):
        return lax.rem(a + i, 4) * sa + lax.rem(b + k, 4) * sb

    a_next, a_prev = {"tp": slot(1, 0)}, {"tp": slot(3, 0)}
    b_next, b_prev = {"tp": slot(0, 1)}, {"tp": slot(0, 3)}
    a_far, b_far = {"tp": slot(2, 0)}, {"tp": slot(0, 2)}
    z_next, z_prev = {"seq": lax.rem(z + 1, 8)}, {"seq": lax.rem(z + 7, 8)}
    other = {"mod": sib}

    barrier = pltpu.get_barrier_semaphore()
    for dev in (a_next, a_prev, a_far, b_next, b_prev, b_far, z_next, z_prev, other):
        pl.semaphore_signal(barrier, inc=1, device_id=dev, device_id_type=MESH)
    pl.semaphore_wait(barrier, 9)

    sent = []
    count = [0]

    def send(src, dst, dev):
        i = count[0]
        count[0] += 1
        copy = pltpu.make_async_remote_copy(
            src_ref=src, dst_ref=dst, send_sem=send_sem.at[i], recv_sem=recv_sem.at[i],
            device_id=dev, device_id_type=MESH)
        copy.start()
        sent.append(copy)
        return copy

    landed = set()

    def arrive(*copies):
        for copy in copies:
            if id(copy) not in landed:
                landed.add(id(copy))
                copy.wait_recv()

    def span_mod(c, block):
        s, h = divmod(c, NH)
        return mod_ref[(s * 8 + z) * TOK + h * R + block * SPAN]

    def pick(flag, one, zero):
        return jnp.where(jnp.full(one.shape, flag, jnp.int32) == 1, one, zero)

    tme = slot(0, 0)
    swap = []
    own_copies = []
    for h in range(NH):
        src = tok_in.at[pl.ds(h * R, R), :]
        dst = tok.at[m * NH + h, tme]
        swap.append(send(src, dst, other))
        cp = pltpu.make_async_copy(src, dst, loc_sem.at[h])
        cp.start()
        own_copies.append(cp)

    w_local = []
    w_remote = []
    for p in range(3):
        cp = pltpu.make_async_copy(
            w_in.at[p, :, pl.ds(pl.multiple_of(m * HD, HD), HD)],
            wcat.at[:, pl.ds(p * HD, HD)], loc_sem.at[NH + p])
        cp.start()
        w_local.append(cp)
        w_remote.append(send(
            w_in.at[p, :, pl.ds(pl.multiple_of(sib * HD, HD), HD)],
            wcat.at[:, pl.ds(384 + p * HD, HD)], other))

    hops = {}

    def gather(c):
        rows = pl.ds(pl.multiple_of(m * H, H), H)
        low = pl.ds(pl.multiple_of(m * H, Q4), Q4)
        high = pl.ds(pl.multiple_of(m * H + Q4, Q4), Q4)

        def put(t, part, dev):
            ref = tok.at[c, t, part]
            return send(ref, ref, dev)

        own = slot(0, 0)
        ar = put(own, rows, a_next)
        al = put(own, rows, a_prev)
        af = put(own, rows, a_far)
        bn, bp = {}, {}
        d2d = hops[c] = {}
        bn[0] = put(own, rows, b_next)
        bp[0] = put(own, rows, b_prev)
        yield
        arrive(ar)
        bn[3] = put(slot(3, 0), rows, b_next)
        bp[3] = put(slot(3, 0), rows, b_prev)
        d2d[3, 0] = put(slot(3, 0), rows, other)
        yield
        arrive(al)
        bn[1] = put(slot(1, 0), rows, b_next)
        bp[1] = put(slot(1, 0), rows, b_prev)
        d2d[1, 0] = put(slot(1, 0), rows, other)
        yield
        arrive(af)
        bn[2] = put(slot(2, 0), rows, b_next)
        bp[2] = put(slot(2, 0), rows, b_prev)
        d2d[2, 0] = put(slot(2, 0), rows, other)
        yield
        g1, g2 = {}, {}
        for i in (0, 3, 1, 2):
            arrive(bn[i])
            g1[i] = put(slot(i, 3), low, b_next)
            d2d[i, 3] = put(slot(i, 3), rows, other)
            arrive(bp[i])
            g2[i] = put(slot(i, 1), high, b_prev)
            d2d[i, 1] = put(slot(i, 1), rows, other)
            yield
        for i in (0, 3, 1, 2):
            arrive(g1[i], g2[i])
            d2d[i, 2] = put(slot(i, 2), rows, other)
            yield

    def unit(c, t):
        x = tok[c, t]
        first = pl.multiple_of(t * W, W)
        g = gain_ref[:, pl.ds(first, W)]
        scaled, squares = [], []
        for k in range(R // SPAN):
            flag = span_mod(c, k)
            xb = x[k * SPAN:(k + 1) * SPAN].astype(F32)
            sq = xb * xb
            squares.append(sq[:, :128] + sq[:, 128:])
            scaled.append((xb * pick(flag, g[1:2], g[0:1])).astype(BF16))
        return (jnp.concatenate(squares, axis=0),
                jnp.dot(jnp.concatenate(scaled, axis=0), wcat[pl.ds(first, W), :],
                        preferred_element_type=F32))

    def units(c, n, where):
        def step(q, carry):
            i, k = where(q)
            squares, part = unit(c, slot(i, k))
            ssq[c] += squares
            acc[c] += part
            return carry
        lax.fori_loop(0, n, step, 0)

    def project(c):
        ssq[c], acc[c] = unit(c, slot(0, 0))
        yield
        d2d = hops[c]
        near = [(i, k) for i in (0, 1, 3) for k in (0, 1, 3) if (i, k) != (0, 0)]

        def grid9(q):
            i, k = lax.div(q, 3), lax.rem(q, 3)
            return i + lax.div(i, 2), k + lax.div(k, 2)

        arrive(*[d2d[p] for p in near])
        units(c, 4, lambda q: grid9(q + 1))
        yield
        units(c, 4, lambda q: grid9(q + 5))
        yield
        arrive(*[d2d[i, k] for i in range(4) for k in range(4) if 2 in (i, k)])
        units(c, 4, lambda q: (2, q))
        yield
        units(c, 3, lambda q: (q + lax.div(q, 2), 2))
        yield
        finish_qkv(c)
        yield

    def finish_qkv(c):
        def step(k, carry):
            r0 = pl.multiple_of(k * SPAN, SPAN)
            flag = span_mod(c, k)
            mine = (jnp.full((SPAN, 3 * HD), flag, jnp.int32) == m)
            block = acc[c, pl.ds(r0, SPAN), :]
            block = jnp.where(mine, block[:, :3 * HD], block[:, 3 * HD:])
            mean = jnp.sum(ssq[c, pl.ds(r0, SPAN), :], axis=1, keepdims=True) * (1.0 / D)
            block = block * lax.rsqrt(mean + epsilon)
            qp, kp, vp = block[:, :HD], block[:, HD:2 * HD], block[:, 2 * HD:]
            qg = pick(flag, hg_ref[1, 0:1], hg_ref[0, 0:1])
            kg = pick(flag, hg_ref[1, 1:2], hg_ref[0, 1:2])
            qm = jnp.mean(qp * qp, axis=1, keepdims=True)
            km = jnp.mean(kp * kp, axis=1, keepdims=True)
            qbuf[pl.ds(c * R + r0, SPAN), :] = (qp * lax.rsqrt(qm + epsilon) * (qg * QSCALE)).astype(BF16)
            kv[c // NH, z, pl.ds(c % NH * R + r0, SPAN), 0:HD] = (kp * lax.rsqrt(km + epsilon) * kg).astype(BF16)
            kv[c // NH, z, pl.ds(c % NH * R + r0, SPAN), HD:2 * HD] = vp.astype(BF16)
            return carry
        lax.fori_loop(0, R // SPAN, step, 0)

    ring = {}

    def zring(c):
        def put(src_z, first, count, dev):
            ref = kv.at[c // NH, lax.rem(src_z, 8), pl.ds(c % NH * R + first, count)]
            return send(ref, ref, dev)

        ring[c, "r", 1] = put(z, 0, R, z_next)
        ring[c, "l", 1] = put(z, 0, R, z_prev)
        yield
        for d in (1, 2, 3):
            count = R if d < 3 else R // 2
            arrive(ring[c, "r", d])
            ring[c, "r", d + 1] = put(z + 8 - d, 0, count, z_next)
            yield
            arrive(ring[c, "l", d])
            ring[c, "l", d + 1] = put(z + d, R - count, count, z_prev)
            yield

    def tile(shard, src, r0, diagonal):
        rows = pl.ds(r0, TQ)
        s = lax.dot_general(qbuf[rows, :], kv[shard, src, :, 0:HD], (((1,), (1,)), ((), ())),
                            preferred_element_type=F32)
        p = jnp.exp2(s)
        if diagonal:
            at = lax.broadcasted_iota(jnp.int32, p.shape, 0) + (r0 - shard * TOK)
            p = jnp.where(lax.broadcasted_iota(jnp.int32, p.shape, 1) <= at, p, 0.0)
        total = p[:, 0:128]
        for k in range(1, TOK // 128):
            total = total + p[:, k * 128:(k + 1) * 128]
        l_acc[rows, :] += total
        o_acc[rows, :] += jnp.dot(p.astype(BF16), kv[shard, src, :, HD:2 * HD], preferred_element_type=F32)

    half = TOK // TQ

    def attend(shard, target, d):
        first = target * half
        if d == 0:
            def own(n, carry):
                tile(shard, z, pl.multiple_of(n * TQ, TQ), shard == target)
                return carry
            lax.fori_loop(first, first + half, own, 0)
            return
        for h in range(NH):
            arrive(ring[shard * NH + h, "r", d], ring[shard * NH + h, "l", d])

        def side(q, carry):
            src = lax.rem(z + 8 - d + q * 2 * d, 8)

            def step(n, inner):
                tile(shard, src, pl.multiple_of(n * TQ, TQ), False)
                return inner
            seen = first + half if shard < target else jnp.where(src < z, first + half, first)
            lax.fori_loop(first, seen, step, 0)
            return carry
        lax.fori_loop(0, 2 if d < 4 else 1, side, 0)

    low_half = pl.ds(0, R // 2)
    high_half = pl.ds(R // 2, R // 2)

    def reduce(c):
        rows = pl.ds(c * R, R)
        total = jnp.sum(l_acc[rows, :], axis=1, keepdims=True)
        att[c, m] = (o_acc[rows, :] / total).astype(BF16)
        ref = att.at[c, m]
        swapped = send(ref, ref, other)
        yield
        arrive(swapped)

        zero = jnp.zeros((SPAN, HD), BF16)
        for n in range(R // SPAN):
            mine = (jnp.full((SPAN, HD), span_mod(c, n), jnp.int32) == m)
            for h in range(2):
                part = att[c, h, n * SPAN:(n + 1) * SPAN, :]
                abuf[c, n * SPAN:(n + 1) * SPAN, h * HD:(h + 1) * HD] = jnp.where(mine, part, zero)
                abuf[c, n * SPAN:(n + 1) * SPAN, 256 + h * HD:256 + (h + 1) * HD] = jnp.where(mine, zero, part)

        def product(g):
            res = jnp.dot(abuf[c], wo[lax.rem(a + g, 4)], preferred_element_type=F32).astype(BF16)
            for k4 in range(4):
                term[c, g, k4] = res[:, k4 * 128:(k4 + 1) * 128]

        product(2)
        s1 = send(term.at[c, 2, :, low_half], r1.at[c, 0], a_next)
        s2 = send(term.at[c, 2, :, high_half], r1.at[c, 1], a_prev)
        yield

        def rest(n, carry):
            product(jnp.where(n == 2, 0, 2 * n + 1))
            return carry
        lax.fori_loop(0, 3, rest, 0)
        yield

        def add(x, y):
            return (x.astype(F32) + y.astype(F32)).astype(BF16)

        arrive(s1)
        msg[c, 0, :, low_half] = add(term[c, 1, :, low_half], r1[c, 0])
        msg[c, 0, :, high_half] = term[c, 1, :, high_half]
        s3 = send(msg.at[c, 0], r2.at[c, 0], a_next)
        yield
        arrive(s2)
        msg[c, 1, :, high_half] = add(term[c, 3, :, high_half], r1[c, 1])
        msg[c, 1, :, low_half] = term[c, 3, :, low_half]
        s4 = send(msg.at[c, 1], r2.at[c, 1], a_prev)
        yield
        arrive(s3, s4)

        def total4(k, carry):
            ubuf[c, k] = (term[c, 0, k].astype(F32) + r2[c, 0, k].astype(F32)
                          + r2[c, 1, k].astype(F32)).astype(BF16)
            return carry

        reach = []
        for k, (i, dev) in enumerate(((2, b_far), (1, b_next), (3, b_prev))):
            to = lax.rem(b + i, 4)
            total4(to, 0)
            reach.append(send(ubuf.at[c, to], r4.at[c, k], dev))
        total4(b, 0)
        yield
        arrive(*reach)
        fin[c] = (ubuf[c, b].astype(F32) + r4[c, 0].astype(F32) + r4[c, 1].astype(F32)
                  + r4[c, 2].astype(F32)).astype(BF16)
        yield

    streams = {}
    for c in range(2 * NH):
        streams["G%d" % c] = gather(c)
        streams["Q%d" % c] = project(c)
        streams["Z%d" % c] = zring(c)
        streams["R%d" % c] = reduce(c)

    wo_local, wo_remote = [], []
    for i in range(4):
        for k in range(4):
            t = i * sa + k * sb
            cp = pltpu.make_async_copy(
                w_out.at[:, pl.ds(pl.multiple_of(t * W + m * HD, HD), HD)],
                wo.at[i, pl.ds(0, 256), pl.ds(k * HD, HD)], loc_sem.at[NH + 3 + i * 4 + k])
            cp.start()
            wo_local.append(cp)
    for cp in own_copies:
        cp.wait()
    arrive(*swap)
    seen = set()
    for name in ORDER:
        if name[0] == "A":
            attend("LU".index(name[1]), "LU".index(name[2]), int(name[3]))
            continue
        if name[0] == "Q" and "Q" not in seen:
            seen.add("Q")
            o_acc[...] = jnp.zeros_like(o_acc)
            l_acc[...] = jnp.zeros_like(l_acc)
            for cp in w_local:
                cp.wait()
            arrive(*w_remote)
        if name == "Z0" and "Z" not in seen:
            seen.add("Z")
            for i in range(4):
                for k in range(4):
                    t = i * sb + k * sa
                    wo_remote.append(send(
                        w_out.at[:, pl.ds(pl.multiple_of(t * W + sib * HD, HD), HD)],
                        wo.at[i, pl.ds(256, 256), pl.ds(k * HD, HD)], other))
        if name[0] == "R" and "R" not in seen:
            seen.add("R")
            for cp in wo_local:
                cp.wait()
            arrive(*wo_remote)
        next(streams[name])

    back = []
    for h in range(NH):
        back.append(send(fin.at[sib * NH + h], fin_in.at[h], other))
    for h in range(NH):
        arrive(back[h])
        own = fin[m * NH + h]
        got = fin_in[h]
        lower = jnp.full(own.shape, m, jnp.int32) == 0
        out_ref[h * R:(h + 1) * R, 0:HD] = jnp.where(lower, own, got)
        out_ref[h * R:(h + 1) * R, HD:2 * HD] = jnp.where(lower, got, own)
    for cp in sent:
        cp.wait_send()


def body(tokens, modality, norm_gain, input_weight, head_gain, output_weight):
    chunks = 2 * NH
    vmem = pl.BlockSpec(memory_space=pltpu.VMEM)
    anywhere = pl.BlockSpec(memory_space=pl.ANY)
    w3 = jnp.transpose(input_weight[0], (1, 0, 2))
    return pl.pallas_call(
        kernel,
        out_shape=jax.ShapeDtypeStruct((TOK, W), BF16),
        in_specs=[pl.BlockSpec(memory_space=pltpu.SMEM), vmem, vmem, anywhere, vmem, anywhere],
        out_specs=vmem,
        scratch_shapes=[
            pltpu.VMEM((chunks, 16, R, W), BF16),
            pltpu.VMEM((D, 6 * HD), BF16),
            pltpu.VMEM((4, 512, 512), BF16),
            pltpu.VMEM((chunks, R, 6 * HD), F32),
            pltpu.VMEM((chunks, R, 128), F32),
            pltpu.VMEM((2 * TOK, HD), BF16),
            pltpu.VMEM((2, 8, TOK, 2 * HD), BF16),
            pltpu.VMEM((2 * TOK, HD), F32),
            pltpu.VMEM((2 * TOK, 128), F32),
            pltpu.VMEM((chunks, 2, R, HD), BF16),
            pltpu.VMEM((chunks, 4, 4, R, 128), BF16),
            pltpu.VMEM((chunks, R, 512), BF16),
            pltpu.VMEM((chunks, 2, 4, R // 2, 128), BF16),
            pltpu.VMEM((chunks, 2, 4, R, 128), BF16),
            pltpu.VMEM((chunks, 2, 4, R, 128), BF16),
            pltpu.VMEM((chunks, 4, R, 128), BF16),
            pltpu.VMEM((chunks, 3, R, 128), BF16),
            pltpu.VMEM((chunks, R, 128), BF16),
            pltpu.VMEM((NH, R, 128), BF16),
            pltpu.SemaphoreType.DMA((N_SEM,)),
            pltpu.SemaphoreType.DMA((N_SEM,)),
            pltpu.SemaphoreType.DMA((NH + 3 + 16,)),
        ],
        compiler_params=pltpu.CompilerParams(
            collective_id=0, has_side_effects=True, vmem_limit_bytes=56 * 1024 * 1024),
    )(modality, tokens, norm_gain, w3, head_gain, output_weight[0])


def solution(mesh):
    in_specs = (
        P(("mod", "seq"), "tp"),
        P(),
        P(),
        P("mod", None, None, "tp"),
        P(),
        P("mod", "tp", None),
    )
    out_specs = P(("mod", "seq"), "tp")
    return jax.shard_map(body, mesh=mesh, in_specs=in_specs, out_specs=out_specs, check_vma=False)
```

```python
import math

import jax
import jax.numpy as jnp
from jax import lax
from jax.experimental import pallas as pl
from jax.experimental.pallas import tpu as pltpu
from jax.sharding import PartitionSpec as P

MESH = pl.DeviceIdType.MESH
F32 = jnp.float32
BF16 = jnp.bfloat16
epsilon = 1e-05
SPAN = 64
HD = 128
TOK = 512
W = 256
D = 4096
NH = 2
R = TOK // NH
H = R // 2
Q4 = H // 2
TQ = 256
ORDER = (
    "G0", "G0", "G0", "Q3", "G0", "G0", "G1", "Q2", "Q1", "Q0", "G0", "G0", "G0", "G0", "Q0", "G1",
    "G1", "Q0", "G1", "G2", "G1", "G0", "G0", "G0", "Q0", "G1", "G1", "Q0", "G1", "Q0", "Z0", "G2",
    "G2", "Q1", "Q1", "G2", "G2", "G1", "G1", "G1", "G1", "G2", "G3", "Q1", "Z0", "Z0", "G2", "Q1",
    "G2", "Q1", "Z1", "G2", "Q2", "G2", "G3", "G3", "Q2", "ALL0", "G3", "G2", "G3", "Z0", "Z0", "G2",
    "Q2", "G3", "G3", "Q2", "Z1", "Z1", "G3", "Q2", "Z2", "G3", "Q3", "Q3", "Z0", "Z0", "G3", "G3",
    "ALL1", "G3", "Q3", "Z1", "Z1", "Q3", "Q3", "Z3", "AUU0", "ALL2", "Z2", "Z2", "ALU0", "ALU1", "ALU2", "Z1",
    "Z1", "ALL3", "ALU3", "Z3", "Z3", "AUU1", "Z2", "Z2", "ALL4", "R1", "R0", "ALU4", "R1", "R1", "Z3", "Z3",
    "R0", "R0", "AUU2", "Z2", "Z2", "R1", "R1", "R0", "R0", "Z3", "Z3", "AUU3", "AUU4", "R3", "R1", "R2",
    "R3", "R3", "R2", "R2", "R0", "R1", "R3", "R3", "R2", "R2", "R0", "R3", "R2", "R3", "R2",
)
LAG = 40
LAST = 7
QSCALE = math.log2(math.e) / math.sqrt(HD)
N_SEM = 256


def kernel(mod_ref, tok_in, gain_ref, w_in, hg_ref, w_out, out_ref,
           tok, wcat, wo, acc, ssq, qbuf, kv, o_acc, l_acc, att, term,
           abuf, r1, r2, msg, ubuf, r4, fin, fin_in,
           send_sem, recv_sem, loc_sem):
    m = lax.axis_index("mod")
    z = lax.axis_index("seq")
    tp = lax.axis_index("tp")
    sib = 1 - m
    sa = 4 - 3 * m
    sb = 1 + 3 * m
    a = lax.rem(lax.div(tp, sa), 4)
    b = lax.rem(lax.div(tp, sb), 4)

    def slot(i, k):
        return lax.rem(a + i, 4) * sa + lax.rem(b + k, 4) * sb

    a_next, a_prev = {"tp": slot(1, 0)}, {"tp": slot(3, 0)}
    b_next, b_prev = {"tp": slot(0, 1)}, {"tp": slot(0, 3)}
    a_far, b_far = {"tp": slot(2, 0)}, {"tp": slot(0, 2)}
    z_next, z_prev = {"seq": lax.rem(z + 1, 8)}, {"seq": lax.rem(z + 7, 8)}
    other = {"mod": sib}

    barrier = pltpu.get_barrier_semaphore()
    for dev in (a_next, a_prev, a_far, b_next, b_prev, b_far, z_next, z_prev, other):
        pl.semaphore_signal(barrier, inc=1, device_id=dev, device_id_type=MESH)
    tme = slot(0, 0)
    own_copies, w_local, wo_local, wo_remote = [], [], [], []
    for h in range(NH):
        cp = pltpu.make_async_copy(tok_in.at[pl.ds(h * R, R), :], tok.at[m * NH + h, tme], loc_sem.at[h])
        cp.start()
        own_copies.append(cp)
    for p in range(3):
        cp = pltpu.make_async_copy(
            w_in.at[p, :, pl.ds(pl.multiple_of(m * HD, HD), HD)],
            wcat.at[:, pl.ds(p * HD, HD)], loc_sem.at[NH + p])
        cp.start()
        w_local.append(cp)
    for i in range(4):
        for k in range(4):
            t = i * sa + k * sb
            cp = pltpu.make_async_copy(
                w_out.at[:, pl.ds(pl.multiple_of(t * W + m * HD, HD), HD)],
                wo.at[i, pl.ds(0, 256), pl.ds(k * HD, HD)], loc_sem.at[NH + 3 + i * 4 + k])
            cp.start()
            wo_local.append(cp)
    o_acc[...] = jnp.zeros_like(o_acc)
    l_acc[...] = jnp.zeros_like(l_acc)
    pl.semaphore_wait(barrier, 9)


    sent = []
    count = [0]

    def send(src, dst, dev):
        i = count[0]
        count[0] += 1
        copy = pltpu.make_async_remote_copy(
            src_ref=src, dst_ref=dst, send_sem=send_sem.at[i], recv_sem=recv_sem.at[i],
            device_id=dev, device_id_type=MESH)
        copy.start()
        sent.append(copy)
        return copy

    landed = set()

    def arrive(*copies):
        for copy in copies:
            if id(copy) not in landed:
                landed.add(id(copy))
                copy.wait_recv()

    def span_mod(c, block):
        s, h = divmod(c, NH)
        return mod_ref[(s * 8 + z) * TOK + h * R + block * SPAN]

    def pick(flag, one, zero):
        return jnp.where(jnp.full(one.shape, flag, jnp.int32) == 1, one, zero)

    swap = []
    w_remote = []
    for h in range(NH):
        swap.append(send(tok_in.at[pl.ds(h * R, R), :], tok.at[m * NH + h, tme], other))
    for p in range(3):
        w_remote.append(send(
            w_in.at[p, :, pl.ds(pl.multiple_of(sib * HD, HD), HD)],
            wcat.at[:, pl.ds(384 + p * HD, HD)], other))

    hops = {}

    def gather(c):
        rows = pl.ds(pl.multiple_of(m * H, H), H)
        low = pl.ds(pl.multiple_of(m * H, Q4), Q4)
        high = pl.ds(pl.multiple_of(m * H + Q4, Q4), Q4)

        def put(t, part, dev):
            ref = tok.at[c, t, part]
            return send(ref, ref, dev)

        own = slot(0, 0)
        ar = put(own, rows, a_next)
        al = put(own, rows, a_prev)
        af = put(own, rows, a_far)
        bn, bp = {}, {}
        d2d = hops[c] = {}
        bn[0] = put(own, rows, b_next)
        bp[0] = put(own, rows, b_prev)
        yield
        arrive(ar)
        bn[3] = put(slot(3, 0), rows, b_next)
        bp[3] = put(slot(3, 0), rows, b_prev)
        d2d[3, 0] = put(slot(3, 0), rows, other)
        yield
        arrive(al)
        bn[1] = put(slot(1, 0), rows, b_next)
        bp[1] = put(slot(1, 0), rows, b_prev)
        d2d[1, 0] = put(slot(1, 0), rows, other)
        yield
        arrive(af)
        bn[2] = put(slot(2, 0), rows, b_next)
        bp[2] = put(slot(2, 0), rows, b_prev)
        d2d[2, 0] = put(slot(2, 0), rows, other)
        yield
        g1, g2 = {}, {}
        for i in (0, 3, 1, 2):
            arrive(bn[i])
            g1[i] = put(slot(i, 3), low, b_next)
            d2d[i, 3] = put(slot(i, 3), rows, other)
            arrive(bp[i])
            g2[i] = put(slot(i, 1), high, b_prev)
            d2d[i, 1] = put(slot(i, 1), rows, other)
            yield
        for i in (0, 3, 1, 2):
            arrive(g1[i], g2[i])
            d2d[i, 2] = put(slot(i, 2), rows, other)
            yield

    def scaled_slice(c, t):
        x = tok[c, t]
        g = gain_ref[:, pl.ds(pl.multiple_of(t * W, W), W)]
        scaled, squares = [], []
        for k in range(R // SPAN):
            flag = span_mod(c, k)
            xb = x[k * SPAN:(k + 1) * SPAN].astype(F32)
            sq = xb * xb
            squares.append(sq[:, :128] + sq[:, 128:])
            scaled.append((xb * pick(flag, g[1:2], g[0:1])).astype(BF16))
        return jnp.concatenate(squares, axis=0), jnp.concatenate(scaled, axis=0)

    def unit(c, *slots):
        parts = [scaled_slice(c, t) for t in slots]
        rows = [wcat[pl.ds(pl.multiple_of(t * W, W), W), :] for t in slots]
        squares = parts[0][0]
        for part in parts[1:]:
            squares = squares + part[0]
        lhs = jnp.concatenate([part[1] for part in parts], axis=1)
        return squares, jnp.dot(lhs, jnp.concatenate(rows, axis=0), preferred_element_type=F32)

    def units(c, n, where):
        def two(q, carry):
            squares, part = unit(c, slot(*where(2 * q)), slot(*where(2 * q + 1)))
            ssq[c] += squares
            acc[c] += part
            return carry
        lax.fori_loop(0, n // 2, two, 0)
        if n % 2:
            squares, part = unit(c, slot(*where(n - 1)))
            ssq[c] += squares
            acc[c] += part

    def project(c):
        ssq[c], acc[c] = unit(c, slot(0, 0))
        yield
        d2d = hops[c]
        near = [(i, k) for i in (0, 1, 3) for k in (0, 1, 3) if (i, k) != (0, 0)]

        def grid9(q):
            i, k = lax.div(q, 3), lax.rem(q, 3)
            return i + lax.div(i, 2), k + lax.div(k, 2)

        arrive(*[d2d[p] for p in near])
        units(c, 4, lambda q: grid9(q + 1))
        yield
        units(c, 4, lambda q: grid9(q + 5))
        yield
        arrive(*[d2d[i, k] for i in range(4) for k in range(4) if 2 in (i, k)])
        units(c, 4, lambda q: (2, q))
        yield
        units(c, 3, lambda q: (q + lax.div(q, 2), 2))
        yield
        finish_qkv(c)
        yield

    def finish_qkv(c):
        def step(k, carry):
            r0 = pl.multiple_of(k * SPAN, SPAN)
            flag = span_mod(c, k)
            mine = (jnp.full((SPAN, 3 * HD), flag, jnp.int32) == m)
            block = acc[c, pl.ds(r0, SPAN), :]
            block = jnp.where(mine, block[:, :3 * HD], block[:, 3 * HD:])
            mean = jnp.sum(ssq[c, pl.ds(r0, SPAN), :], axis=1, keepdims=True) * (1.0 / D)
            block = block * lax.rsqrt(mean + epsilon)
            qp, kp, vp = block[:, :HD], block[:, HD:2 * HD], block[:, 2 * HD:]
            qg = pick(flag, hg_ref[1, 0:1], hg_ref[0, 0:1])
            kg = pick(flag, hg_ref[1, 1:2], hg_ref[0, 1:2])
            qm = jnp.mean(qp * qp, axis=1, keepdims=True)
            km = jnp.mean(kp * kp, axis=1, keepdims=True)
            qbuf[pl.ds(c * R + r0, SPAN), :] = (qp * lax.rsqrt(qm + epsilon) * (qg * QSCALE)).astype(BF16)
            kv[c // NH, z, pl.ds(c % NH * R + r0, SPAN), 0:HD] = (kp * lax.rsqrt(km + epsilon) * kg).astype(BF16)
            kv[c // NH, z, pl.ds(c % NH * R + r0, SPAN), HD:2 * HD] = vp.astype(BF16)
            return carry
        lax.fori_loop(0, R // SPAN, step, 0)

    ring = {}

    def zring(c):
        def put(src_z, first, count, dev):
            ref = kv.at[c // NH, lax.rem(src_z, 8), pl.ds(c % NH * R + first, count)]
            return send(ref, ref, dev)

        ring[c, "r", 1] = put(z, 0, R, z_next)
        ring[c, "l", 1] = put(z, 0, R, z_prev)
        yield
        for d in (1, 2, 3):
            count = R if d < 3 else R // 2
            arrive(ring[c, "r", d])
            ring[c, "r", d + 1] = put(z + 8 - d, 0, count, z_next)
            yield
            arrive(ring[c, "l", d])
            ring[c, "l", d + 1] = put(z + d, R - count, count, z_prev)
            yield

    def tile(shard, src, r0, diagonal):
        rows = pl.ds(r0, TQ)
        s = lax.dot_general(qbuf[rows, :], kv[shard, src, :, 0:HD], (((1,), (1,)), ((), ())),
                            preferred_element_type=F32)
        p = jnp.exp2(s)
        if diagonal:
            at = lax.broadcasted_iota(jnp.int32, p.shape, 0) + (r0 - shard * TOK)
            p = jnp.where(lax.broadcasted_iota(jnp.int32, p.shape, 1) <= at, p, 0.0)
        total = p[:, 0:128]
        for k in range(1, TOK // 128):
            total = total + p[:, k * 128:(k + 1) * 128]
        l_acc[rows, :] += total
        o_acc[rows, :] += jnp.dot(p.astype(BF16), kv[shard, src, :, HD:2 * HD], preferred_element_type=F32)

    half = TOK // TQ

    def attend(shard, target, d):
        first = target * half
        if d == 0:
            def own(n, carry):
                tile(shard, z, pl.multiple_of(n * TQ, TQ), shard == target)
                return carry
            lax.fori_loop(first, first + half, own, 0)
            return
        for h in range(NH):
            arrive(ring[shard * NH + h, "r", d], ring[shard * NH + h, "l", d])

        def side(q, carry):
            src = lax.rem(z + 8 - d + q * 2 * d, 8)

            def step(n, inner):
                tile(shard, src, pl.multiple_of(n * TQ, TQ), False)
                return inner
            seen = first + half if shard < target else jnp.where(src < z, first + half, first)
            lax.fori_loop(first, seen, step, 0)
            return carry
        lax.fori_loop(0, 2 if d < 4 else 1, side, 0)

    low_half = pl.ds(0, R // 2)
    high_half = pl.ds(R // 2, R // 2)

    def reduce(c):
        rows = pl.ds(c * R, R)
        total = jnp.sum(l_acc[rows, :], axis=1, keepdims=True)
        att[c, m] = (o_acc[rows, :] / total).astype(BF16)
        ref = att.at[c, m]
        swapped = send(ref, ref, other)
        yield
        arrive(swapped)

        zero = jnp.zeros((SPAN, HD), BF16)
        for n in range(R // SPAN):
            mine = (jnp.full((SPAN, HD), span_mod(c, n), jnp.int32) == m)
            for h in range(2):
                part = att[c, h, n * SPAN:(n + 1) * SPAN, :]
                abuf[c, n * SPAN:(n + 1) * SPAN, h * HD:(h + 1) * HD] = jnp.where(mine, part, zero)
                abuf[c, n * SPAN:(n + 1) * SPAN, 256 + h * HD:256 + (h + 1) * HD] = jnp.where(mine, zero, part)

        def product(g):
            res = jnp.dot(abuf[c], wo[lax.rem(a + g, 4)], preferred_element_type=F32).astype(BF16)
            for k4 in range(4):
                term[c, g, k4] = res[:, k4 * 128:(k4 + 1) * 128]

        product(2)
        s1 = send(term.at[c, 2, :, low_half], r1.at[c, 0], a_next)
        s2 = send(term.at[c, 2, :, high_half], r1.at[c, 1], a_prev)
        yield

        def rest(n, carry):
            product(jnp.where(n == 2, 0, 2 * n + 1))
            return carry
        lax.fori_loop(0, 3, rest, 0)
        yield

        def add(x, y):
            return (x.astype(F32) + y.astype(F32)).astype(BF16)

        arrive(s1)
        msg[c, 0, :, low_half] = add(term[c, 1, :, low_half], r1[c, 0])
        msg[c, 0, :, high_half] = term[c, 1, :, high_half]
        s3 = send(msg.at[c, 0], r2.at[c, 0], a_next)
        yield
        arrive(s2)
        msg[c, 1, :, high_half] = add(term[c, 3, :, high_half], r1[c, 1])
        msg[c, 1, :, low_half] = term[c, 3, :, low_half]
        s4 = send(msg.at[c, 1], r2.at[c, 1], a_prev)
        yield
        arrive(s3, s4)

        def total4(k, carry):
            ubuf[c, k] = (term[c, 0, k].astype(F32) + r2[c, 0, k].astype(F32)
                          + r2[c, 1, k].astype(F32)).astype(BF16)
            return carry

        reach = []
        for k, (i, dev) in enumerate(((2, b_far), (1, b_next), (3, b_prev))):
            to = lax.rem(b + i, 4)
            total4(to, 0)
            reach.append(send(ubuf.at[c, to], r4.at[c, k], dev))
        total4(b, 0)
        yield
        arrive(*reach)
        fin[c] = (ubuf[c, b].astype(F32) + r4[c, 0].astype(F32) + r4[c, 1].astype(F32)
                  + r4[c, 2].astype(F32)).astype(BF16)
        yield

    streams = {}
    for c in range(2 * NH):
        streams["G%d" % c] = gather(c)
        streams["Q%d" % c] = project(c)
        streams["Z%d" % c] = zring(c)
        streams["R%d" % c] = reduce(c)

    for cp in own_copies:
        cp.wait()
    arrive(*swap)
    seen = set()
    issued = []
    turns = {}
    back = {}
    retired = 0
    for number, name in enumerate(ORDER):
        issued.append(len(sent))
        if number >= LAG:
            while retired < issued[number - LAG]:
                sent[retired].wait_send()
                retired += 1
        if name[0] == "A":
            attend("LU".index(name[1]), "LU".index(name[2]), int(name[3]))
            continue
        if name[0] == "Q" and "Q" not in seen:
            seen.add("Q")
            for cp in w_local:
                cp.wait()
            arrive(*w_remote)
        if name == "Z0" and "Z" not in seen:
            seen.add("Z")
            for i in range(4):
                for k in range(4):
                    t = i * sb + k * sa
                    wo_remote.append(send(
                        w_out.at[:, pl.ds(pl.multiple_of(t * W + sib * HD, HD), HD)],
                        wo.at[i, pl.ds(256, 256), pl.ds(k * HD, HD)], other))
        if name[0] == "R" and "R" not in seen:
            seen.add("R")
            for cp in wo_local:
                cp.wait()
            arrive(*wo_remote)
        next(streams[name])
        if name[0] == "R":
            turns[name] = turns.get(name, 0) + 1
            h = int(name[1]) % NH
            if turns.get("R%d" % h) == LAST and turns.get("R%d" % (h + NH)) == LAST:
                back[h] = send(fin.at[sib * NH + h], fin_in.at[h], other)

    for h in range(NH):
        arrive(back[h])
        own = fin[m * NH + h]
        got = fin_in[h]
        lower = jnp.full(own.shape, m, jnp.int32) == 0
        out_ref[h * R:(h + 1) * R, 0:HD] = jnp.where(lower, own, got)
        out_ref[h * R:(h + 1) * R, HD:2 * HD] = jnp.where(lower, got, own)
    for cp in sent[retired:]:
        cp.wait_send()


def body(tokens, modality, norm_gain, input_weight, head_gain, output_weight):
    chunks = 2 * NH
    vmem = pl.BlockSpec(memory_space=pltpu.VMEM)
    anywhere = pl.BlockSpec(memory_space=pl.ANY)
    w3 = jnp.transpose(input_weight[0], (1, 0, 2))
    return pl.pallas_call(
        kernel,
        out_shape=jax.ShapeDtypeStruct((TOK, W), BF16),
        in_specs=[pl.BlockSpec(memory_space=pltpu.SMEM), vmem, vmem, anywhere, vmem, anywhere],
        out_specs=vmem,
        scratch_shapes=[
            pltpu.VMEM((chunks, 16, R, W), BF16),
            pltpu.VMEM((D, 6 * HD), BF16),
            pltpu.VMEM((4, 512, 512), BF16),
            pltpu.VMEM((chunks, R, 6 * HD), F32),
            pltpu.VMEM((chunks, R, 128), F32),
            pltpu.VMEM((2 * TOK, HD), BF16),
            pltpu.VMEM((2, 8, TOK, 2 * HD), BF16),
            pltpu.VMEM((2 * TOK, HD), F32),
            pltpu.VMEM((2 * TOK, 128), F32),
            pltpu.VMEM((chunks, 2, R, HD), BF16),
            pltpu.VMEM((chunks, 4, 4, R, 128), BF16),
            pltpu.VMEM((chunks, R, 512), BF16),
            pltpu.VMEM((chunks, 2, 4, R // 2, 128), BF16),
            pltpu.VMEM((chunks, 2, 4, R, 128), BF16),
            pltpu.VMEM((chunks, 2, 4, R, 128), BF16),
            pltpu.VMEM((chunks, 4, R, 128), BF16),
            pltpu.VMEM((chunks, 3, R, 128), BF16),
            pltpu.VMEM((chunks, R, 128), BF16),
            pltpu.VMEM((NH, R, 128), BF16),
            pltpu.SemaphoreType.DMA((N_SEM,)),
            pltpu.SemaphoreType.DMA((N_SEM,)),
            pltpu.SemaphoreType.DMA((NH + 3 + 16,)),
        ],
        compiler_params=pltpu.CompilerParams(
            collective_id=0, has_side_effects=True, vmem_limit_bytes=56 * 1024 * 1024),
    )(modality, tokens, norm_gain, w3, head_gain, output_weight[0])


def solution(mesh):
    in_specs = (
        P(("mod", "seq"), "tp"),
        P(),
        P(),
        P("mod", None, None, "tp"),
        P(),
        P("mod", "tp", None),
    )
    out_specs = P(("mod", "seq"), "tp")
    return jax.shard_map(body, mesh=mesh, in_specs=in_specs, out_specs=out_specs, check_vma=False)
```

```python
import math

import jax
import jax.numpy as jnp
from jax import lax
from jax.experimental import pallas as pl
from jax.experimental.pallas import tpu as pltpu
from jax.sharding import PartitionSpec as P

MESH = pl.DeviceIdType.MESH
F32 = jnp.float32
BF16 = jnp.bfloat16
epsilon = 1e-05
SPAN = 64
HD = 128
TOK = 512
W = 256
D = 4096
NH = 2
R = TOK // NH
H = R // 2
Q4 = H // 2
TQ = 256
ORDER = (
    "G0", "G0", "G0", "Q0", "G0", "G0", "G1", "Q2", "Q3", "Q1", "G0", "G0", "G0", "G0", "Q0", "Q0",
    "G1", "G1", "G1", "G1", "G2", "G0", "G0", "G0", "Q0", "Q0", "Q0", "Z0", "G1", "G1", "G1", "G1",
    "Q1", "G2", "G2", "Q1", "G2", "G2", "G1", "G1", "G1", "Z0", "Z0", "Q1", "G2", "Q1", "G2", "G3",
    "Q1", "Z1", "G2", "G2", "ALL0", "Q2", "G2", "Q2", "Z0", "Z0", "G2", "G3", "G3", "G3", "G3", "G2",
    "Z1", "Z1", "ALL1", "G3", "Q2", "G3", "G3", "Z0", "Z0", "G3", "Q2", "Q2", "Z2", "Q3", "G3", "Q3",
    "Z1", "Z1", "G3", "G3", "ALL2", "Q3", "Q3", "Q3", "Z3", "Z2", "Z2", "ALU2", "ALU0", "ALU1", "Z1", "Z1",
    "ALL3", "ALU3", "Z3", "Z3", "AUU1", "AUU0", "Z2", "Z2", "ALL4", "R0", "R1", "ALU4", "R0", "R0", "Z3", "Z3",
    "R1", "R1", "AUU2", "Z2", "Z2", "R0", "R0", "R1", "R1", "Z3", "Z3", "AUU3", "AUU4", "R0", "R2", "R3",
    "R2", "R2", "R3", "R3", "R0", "R1", "R2", "R2", "R3", "R3", "R1", "R2", "R3", "R2", "R3",
)
LAG = 40
LAST = 7
QSCALE = math.log2(math.e) / math.sqrt(HD)
N_SEM = 256


def kernel(mod_ref, tok_in, gain_ref, w_in, hg_ref, w_out, out_ref,
           tok, wcat, wo, acc, ssq, qbuf, kv, o_acc, l_acc, att, term,
           abuf, r1, r2, msg, ubuf, r4, fin, fin_in,
           send_sem, recv_sem, loc_sem):
    m = lax.axis_index("mod")
    z = lax.axis_index("seq")
    tp = lax.axis_index("tp")
    sib = 1 - m
    sa = 4 - 3 * m
    sb = 1 + 3 * m
    a = lax.rem(lax.div(tp, sa), 4)
    b = lax.rem(lax.div(tp, sb), 4)

    def slot(i, k):
        return lax.rem(a + i, 4) * sa + lax.rem(b + k, 4) * sb

    a_next, a_prev = {"tp": slot(1, 0)}, {"tp": slot(3, 0)}
    b_next, b_prev = {"tp": slot(0, 1)}, {"tp": slot(0, 3)}
    a_far, b_far = {"tp": slot(2, 0)}, {"tp": slot(0, 2)}
    z_next, z_prev = {"seq": lax.rem(z + 1, 8)}, {"seq": lax.rem(z + 7, 8)}
    other = {"mod": sib}

    barrier = pltpu.get_barrier_semaphore()
    for dev in (a_next, a_prev, a_far, b_next, b_prev, b_far, z_next, z_prev, other):
        pl.semaphore_signal(barrier, inc=1, device_id=dev, device_id_type=MESH)
    tme = slot(0, 0)
    own_copies, w_local, wo_local, wo_remote = [], [], [], []
    for h in range(NH):
        cp = pltpu.make_async_copy(tok_in.at[pl.ds(h * R, R), :], tok.at[m * NH + h, tme], loc_sem.at[h])
        cp.start()
        own_copies.append(cp)
    for p in range(3):
        cp = pltpu.make_async_copy(
            w_in.at[p, :, pl.ds(pl.multiple_of(m * HD, HD), HD)],
            wcat.at[:, pl.ds(p * HD, HD)], loc_sem.at[NH + p])
        cp.start()
        w_local.append(cp)
    for i in range(4):
        for k in range(4):
            t = i * sa + k * sb
            cp = pltpu.make_async_copy(
                w_out.at[:, pl.ds(pl.multiple_of(t * W + m * HD, HD), HD)],
                wo.at[i, pl.ds(0, 256), pl.ds(k * HD, HD)], loc_sem.at[NH + 3 + i * 4 + k])
            cp.start()
            wo_local.append(cp)
    o_acc[...] = jnp.zeros_like(o_acc)
    l_acc[...] = jnp.zeros_like(l_acc)
    pl.semaphore_wait(barrier, 9)


    sent = []
    count = [0]

    def send(src, dst, dev):
        i = count[0]
        count[0] += 1
        copy = pltpu.make_async_remote_copy(
            src_ref=src, dst_ref=dst, send_sem=send_sem.at[i], recv_sem=recv_sem.at[i],
            device_id=dev, device_id_type=MESH)
        copy.start()
        sent.append(copy)
        return copy

    landed = set()

    def arrive(*copies):
        for copy in copies:
            if id(copy) not in landed:
                landed.add(id(copy))
                copy.wait_recv()

    def span_mod(c, block):
        s, h = divmod(c, NH)
        return mod_ref[(s * 8 + z) * TOK + h * R + block * SPAN]

    def pick(flag, one, zero):
        return jnp.where(jnp.full(one.shape, flag, jnp.int32) == 1, one, zero)

    swap = []
    w_remote = []
    for h in range(NH):
        swap.append(send(tok_in.at[pl.ds(h * R, R), :], tok.at[m * NH + h, tme], other))
    for p in range(3):
        w_remote.append(send(
            w_in.at[p, :, pl.ds(pl.multiple_of(sib * HD, HD), HD)],
            wcat.at[:, pl.ds(384 + p * HD, HD)], other))

    hops = {}

    def gather(c):
        rows = pl.ds(pl.multiple_of(m * H, H), H)
        low = pl.ds(pl.multiple_of(m * H, Q4), Q4)
        high = pl.ds(pl.multiple_of(m * H + Q4, Q4), Q4)

        def put(t, part, dev):
            ref = tok.at[c, t, part]
            return send(ref, ref, dev)

        own = slot(0, 0)
        ar = put(own, rows, a_next)
        al = put(own, rows, a_prev)
        af = put(own, rows, a_far)
        bn, bp = {}, {}
        d2d = hops[c] = {}
        bn[0] = put(own, rows, b_next)
        bp[0] = put(own, rows, b_prev)
        yield
        arrive(ar)
        bn[3] = put(slot(3, 0), rows, b_next)
        bp[3] = put(slot(3, 0), rows, b_prev)
        d2d[3, 0] = put(slot(3, 0), rows, other)
        yield
        arrive(al)
        bn[1] = put(slot(1, 0), rows, b_next)
        bp[1] = put(slot(1, 0), rows, b_prev)
        d2d[1, 0] = put(slot(1, 0), rows, other)
        yield
        arrive(af)
        bn[2] = put(slot(2, 0), rows, b_next)
        bp[2] = put(slot(2, 0), rows, b_prev)
        d2d[2, 0] = put(slot(2, 0), rows, other)
        yield
        g1, g2 = {}, {}
        for i in (0, 3, 1, 2):
            arrive(bn[i])
            g1[i] = put(slot(i, 3), low, b_next)
            d2d[i, 3] = put(slot(i, 3), rows, other)
            arrive(bp[i])
            g2[i] = put(slot(i, 1), high, b_prev)
            d2d[i, 1] = put(slot(i, 1), rows, other)
            yield
        for i in (0, 3, 1, 2):
            arrive(g1[i], g2[i])
            d2d[i, 2] = put(slot(i, 2), rows, other)
            yield

    def scaled_slice(c, t):
        x = tok[c, t]
        g = gain_ref[:, pl.ds(pl.multiple_of(t * W, W), W)]
        scaled, squares = [], []
        for k in range(R // SPAN):
            flag = span_mod(c, k)
            xb = x[k * SPAN:(k + 1) * SPAN].astype(F32)
            sq = xb * xb
            squares.append(sq[:, :128] + sq[:, 128:])
            scaled.append((xb * pick(flag, g[1:2], g[0:1])).astype(BF16))
        return jnp.concatenate(squares, axis=0), jnp.concatenate(scaled, axis=0)

    def unit(c, *slots):
        parts = [scaled_slice(c, t) for t in slots]
        rows = [wcat[pl.ds(pl.multiple_of(t * W, W), W), :] for t in slots]
        squares = parts[0][0]
        for part in parts[1:]:
            squares = squares + part[0]
        lhs = jnp.concatenate([part[1] for part in parts], axis=1)
        return squares, jnp.dot(lhs, jnp.concatenate(rows, axis=0), preferred_element_type=F32)

    def units(c, n, where):
        def two(q, carry):
            squares, part = unit(c, slot(*where(2 * q)), slot(*where(2 * q + 1)))
            ssq[c] += squares
            acc[c] += part
            return carry
        lax.fori_loop(0, n // 2, two, 0)
        if n % 2:
            squares, part = unit(c, slot(*where(n - 1)))
            ssq[c] += squares
            acc[c] += part

    def project(c):
        ssq[c], acc[c] = unit(c, slot(0, 0))
        yield
        d2d = hops[c]
        near = [(i, k) for i in (0, 1, 3) for k in (0, 1, 3) if (i, k) != (0, 0)]

        def grid9(q):
            i, k = lax.div(q, 3), lax.rem(q, 3)
            return i + lax.div(i, 2), k + lax.div(k, 2)

        arrive(*[d2d[p] for p in near])
        units(c, 4, lambda q: grid9(q + 1))
        yield
        units(c, 4, lambda q: grid9(q + 5))
        yield
        arrive(*[d2d[i, k] for i in range(4) for k in range(4) if 2 in (i, k)])
        units(c, 4, lambda q: (2, q))
        yield
        units(c, 3, lambda q: (q + lax.div(q, 2), 2))
        yield
        finish_qkv(c)
        yield

    def finish_qkv(c):
        def step(k, carry):
            r0 = pl.multiple_of(k * SPAN, SPAN)
            flag = span_mod(c, k)
            mine = (jnp.full((SPAN, 3 * HD), flag, jnp.int32) == m)
            block = acc[c, pl.ds(r0, SPAN), :]
            block = jnp.where(mine, block[:, :3 * HD], block[:, 3 * HD:])
            mean = jnp.sum(ssq[c, pl.ds(r0, SPAN), :], axis=1, keepdims=True) * (1.0 / D)
            block = block * lax.rsqrt(mean + epsilon)
            qp, kp, vp = block[:, :HD], block[:, HD:2 * HD], block[:, 2 * HD:]
            qg = pick(flag, hg_ref[1, 0:1], hg_ref[0, 0:1])
            kg = pick(flag, hg_ref[1, 1:2], hg_ref[0, 1:2])
            qm = jnp.mean(qp * qp, axis=1, keepdims=True)
            km = jnp.mean(kp * kp, axis=1, keepdims=True)
            qbuf[pl.ds(c * R + r0, SPAN), :] = (qp * lax.rsqrt(qm + epsilon) * (qg * QSCALE)).astype(BF16)
            kv[c // NH, z, pl.ds(c % NH * R + r0, SPAN), 0:HD] = (kp * lax.rsqrt(km + epsilon) * kg).astype(BF16)
            kv[c // NH, z, pl.ds(c % NH * R + r0, SPAN), HD:2 * HD] = vp.astype(BF16)
            return carry
        lax.fori_loop(0, R // SPAN, step, 0)

    ring = {}

    def zring(c):
        def put(src_z, first, count, dev):
            ref = kv.at[c // NH, lax.rem(src_z, 8), pl.ds(c % NH * R + first, count)]
            return send(ref, ref, dev)

        ring[c, "r", 1] = put(z, 0, R, z_next)
        ring[c, "l", 1] = put(z, 0, R, z_prev)
        yield
        for d in (1, 2, 3):
            count = R if d < 3 else R // 2
            arrive(ring[c, "r", d])
            ring[c, "r", d + 1] = put(z + 8 - d, 0, count, z_next)
            yield
            arrive(ring[c, "l", d])
            ring[c, "l", d + 1] = put(z + d, R - count, count, z_prev)
            yield

    def tile(shard, src, r0, diagonal):
        rows = pl.ds(r0, TQ)
        s = lax.dot_general(qbuf[rows, :], kv[shard, src, :, 0:HD], (((1,), (1,)), ((), ())),
                            preferred_element_type=F32)
        p = jnp.exp2(s)
        if diagonal:
            at = lax.broadcasted_iota(jnp.int32, p.shape, 0) + (r0 - shard * TOK)
            p = jnp.where(lax.broadcasted_iota(jnp.int32, p.shape, 1) <= at, p, 0.0)
        total = p[:, 0:128]
        for k in range(1, TOK // 128):
            total = total + p[:, k * 128:(k + 1) * 128]
        l_acc[rows, :] += total
        o_acc[rows, :] += jnp.dot(p.astype(BF16), kv[shard, src, :, HD:2 * HD], preferred_element_type=F32)

    half = TOK // TQ

    def attend(shard, target, d):
        first = target * half
        if d == 0:
            def own(n, carry):
                tile(shard, z, pl.multiple_of(n * TQ, TQ), shard == target)
                return carry
            lax.fori_loop(first, first + half, own, 0)
            return
        for h in range(NH):
            arrive(ring[shard * NH + h, "r", d], ring[shard * NH + h, "l", d])

        def side(q, carry):
            src = lax.rem(z + 8 - d + q * 2 * d, 8)

            def step(n, inner):
                tile(shard, src, pl.multiple_of(n * TQ, TQ), False)
                return inner
            seen = first + half if shard < target else jnp.where(src < z, first + half, first)
            lax.fori_loop(first, seen, step, 0)
            return carry
        lax.fori_loop(0, 2 if d < 4 else 1, side, 0)

    low_half = pl.ds(0, R // 2)
    high_half = pl.ds(R // 2, R // 2)

    def reduce(c):
        rows = pl.ds(c * R, R)
        total = jnp.sum(l_acc[rows, :], axis=1, keepdims=True)
        att[c, m] = (o_acc[rows, :] / total).astype(BF16)
        ref = att.at[c, m]
        swapped = send(ref, ref, other)
        yield
        arrive(swapped)

        zero = jnp.zeros((SPAN, HD), BF16)
        for n in range(R // SPAN):
            mine = (jnp.full((SPAN, HD), span_mod(c, n), jnp.int32) == m)
            for h in range(2):
                part = att[c, h, n * SPAN:(n + 1) * SPAN, :]
                abuf[c, n * SPAN:(n + 1) * SPAN, h * HD:(h + 1) * HD] = jnp.where(mine, part, zero)
                abuf[c, n * SPAN:(n + 1) * SPAN, 256 + h * HD:256 + (h + 1) * HD] = jnp.where(mine, zero, part)

        def product(g):
            res = jnp.dot(abuf[c], wo[lax.rem(a + g, 4)], preferred_element_type=F32).astype(BF16)
            for k4 in range(4):
                term[c, g, k4] = res[:, k4 * 128:(k4 + 1) * 128]

        product(2)
        s1 = send(term.at[c, 2, :, low_half], r1.at[c, 0], a_next)
        s2 = send(term.at[c, 2, :, high_half], r1.at[c, 1], a_prev)
        yield

        def rest(n, carry):
            product(jnp.where(n == 2, 0, 2 * n + 1))
            return carry
        lax.fori_loop(0, 3, rest, 0)
        yield

        def add(x, y):
            return (x.astype(F32) + y.astype(F32)).astype(BF16)

        arrive(s1)
        msg[c, 0, :, low_half] = add(term[c, 1, :, low_half], r1[c, 0])
        msg[c, 0, :, high_half] = term[c, 1, :, high_half]
        s3 = send(msg.at[c, 0], r2.at[c, 0], a_next)
        yield
        arrive(s2)
        msg[c, 1, :, high_half] = add(term[c, 3, :, high_half], r1[c, 1])
        msg[c, 1, :, low_half] = term[c, 3, :, low_half]
        s4 = send(msg.at[c, 1], r2.at[c, 1], a_prev)
        yield
        arrive(s3, s4)

        def total4(k, carry):
            ubuf[c, k] = (term[c, 0, k].astype(F32) + r2[c, 0, k].astype(F32)
                          + r2[c, 1, k].astype(F32)).astype(BF16)
            return carry

        reach = []
        for k, (i, dev) in enumerate(((2, b_far), (1, b_next), (3, b_prev))):
            to = lax.rem(b + i, 4)
            total4(to, 0)
            reach.append(send(ubuf.at[c, to], r4.at[c, k], dev))
        total4(b, 0)
        yield
        arrive(*reach)
        fin[c] = (ubuf[c, b].astype(F32) + r4[c, 0].astype(F32) + r4[c, 1].astype(F32)
                  + r4[c, 2].astype(F32)).astype(BF16)
        yield

    streams = {}
    for c in range(2 * NH):
        streams["G%d" % c] = gather(c)
        streams["Q%d" % c] = project(c)
        streams["Z%d" % c] = zring(c)
        streams["R%d" % c] = reduce(c)

    for cp in own_copies:
        cp.wait()
    arrive(*swap)
    seen = set()
    issued = []
    turns = {}
    back = {}
    retired = 0
    for number, name in enumerate(ORDER):
        issued.append(len(sent))
        if number >= LAG:
            while retired < issued[number - LAG]:
                sent[retired].wait_send()
                retired += 1
        if name[0] == "A":
            attend("LU".index(name[1]), "LU".index(name[2]), int(name[3]))
            continue
        if name[0] == "Q" and "Q" not in seen:
            seen.add("Q")
            for cp in w_local:
                cp.wait()
            arrive(*w_remote)
        if name == "Z0" and "Z" not in seen:
            seen.add("Z")
            for i in range(4):
                for k in range(4):
                    t = i * sb + k * sa
                    wo_remote.append(send(
                        w_out.at[:, pl.ds(pl.multiple_of(t * W + sib * HD, HD), HD)],
                        wo.at[i, pl.ds(256, 256), pl.ds(k * HD, HD)], other))
        if name[0] == "R" and "R" not in seen:
            seen.add("R")
            for cp in wo_local:
                cp.wait()
            arrive(*wo_remote)
        next(streams[name])
        if name[0] == "R":
            turns[name] = turns.get(name, 0) + 1
            h = int(name[1]) % NH
            if turns.get("R%d" % h) == LAST and turns.get("R%d" % (h + NH)) == LAST:
                back[h] = send(fin.at[sib * NH + h], fin_in.at[h], other)

    for h in range(NH):
        arrive(back[h])
        own = fin[m * NH + h]
        got = fin_in[h]
        lower = jnp.full(own.shape, m, jnp.int32) == 0
        out_ref[h * R:(h + 1) * R, 0:HD] = jnp.where(lower, own, got)
        out_ref[h * R:(h + 1) * R, HD:2 * HD] = jnp.where(lower, got, own)
    for cp in sent[retired:]:
        cp.wait_send()


def body(tokens, modality, norm_gain, input_weight, head_gain, output_weight):
    chunks = 2 * NH
    vmem = pl.BlockSpec(memory_space=pltpu.VMEM)
    anywhere = pl.BlockSpec(memory_space=pl.ANY)
    w3 = jnp.transpose(input_weight[0], (1, 0, 2))
    return pl.pallas_call(
        kernel,
        out_shape=jax.ShapeDtypeStruct((TOK, W), BF16),
        in_specs=[pl.BlockSpec(memory_space=pltpu.SMEM), vmem, vmem, anywhere, vmem, anywhere],
        out_specs=vmem,
        scratch_shapes=[
            pltpu.VMEM((chunks, 16, R, W), BF16),
            pltpu.VMEM((D, 6 * HD), BF16),
            pltpu.VMEM((4, 512, 512), BF16),
            pltpu.VMEM((chunks, R, 6 * HD), F32),
            pltpu.VMEM((chunks, R, 128), F32),
            pltpu.VMEM((2 * TOK, HD), BF16),
            pltpu.VMEM((2, 8, TOK, 2 * HD), BF16),
            pltpu.VMEM((2 * TOK, HD), F32),
            pltpu.VMEM((2 * TOK, 128), F32),
            pltpu.VMEM((chunks, 2, R, HD), BF16),
            pltpu.VMEM((chunks, 4, 4, R, 128), BF16),
            pltpu.VMEM((chunks, R, 512), BF16),
            pltpu.VMEM((chunks, 2, 4, R // 2, 128), BF16),
            pltpu.VMEM((chunks, 2, 4, R, 128), BF16),
            pltpu.VMEM((chunks, 2, 4, R, 128), BF16),
            pltpu.VMEM((chunks, 4, R, 128), BF16),
            pltpu.VMEM((chunks, 3, R, 128), BF16),
            pltpu.VMEM((chunks, R, 128), BF16),
            pltpu.VMEM((NH, R, 128), BF16),
            pltpu.SemaphoreType.DMA((N_SEM,)),
            pltpu.SemaphoreType.DMA((N_SEM,)),
            pltpu.SemaphoreType.DMA((NH + 3 + 16,)),
        ],
        compiler_params=pltpu.CompilerParams(
            collective_id=0, has_side_effects=True, vmem_limit_bytes=56 * 1024 * 1024),
    )(modality, tokens, norm_gain, w3, head_gain, output_weight[0])


def solution(mesh):
    in_specs = (
        P(("mod", "seq"), "tp"),
        P(),
        P(),
        P("mod", None, None, "tp"),
        P(),
        P("mod", "tp", None),
    )
    out_specs = P(("mod", "seq"), "tp")
    return jax.shard_map(body, mesh=mesh, in_specs=in_specs, out_specs=out_specs, check_vma=False)
```

```python
import math

import jax
import jax.numpy as jnp
from jax import lax
from jax.experimental import pallas as pl
from jax.experimental.pallas import tpu as pltpu
from jax.sharding import PartitionSpec as P

MESH = pl.DeviceIdType.MESH
F32 = jnp.float32
BF16 = jnp.bfloat16
epsilon = 1e-05
SPAN = 64
HD = 128
TOK = 512
W = 256
D = 4096
NH = 2
R = TOK // NH
H = R // 2
Q4 = H // 2
TQ = 256
ORDER = (
    "G0", "G0", "G0", "Q0", "G0", "G0", "G1", "Q2", "Q3", "Q1", "G0", "G0", "G0", "G0", "Q0", "Q0",
    "G1", "G1", "G1", "G1", "G2", "G0", "G0", "G0", "Q0", "Q0", "Q0", "Z0", "G1", "G1", "G1", "G1",
    "Q1", "G2", "G2", "Q1", "G2", "G2", "G1", "G1", "G1", "Z0", "Z0", "Q1", "G2", "Q1", "G2", "G3",
    "Q1", "Z1", "G2", "G2", "ALL0", "Q2", "G2", "Q2", "Z0", "Z0", "G2", "G3", "G3", "G3", "G3", "G2",
    "Z1", "Z1", "ALL1", "G3", "Q2", "G3", "G3", "Z0", "Z0", "G3", "Q2", "Q2", "Z2", "Q3", "G3", "Q3",
    "Z1", "Z1", "G3", "G3", "ALL2", "Q3", "Q3", "Q3", "Z3", "Z2", "Z2", "ALU2", "ALU0", "ALU1", "Z1", "Z1",
    "ALL3", "ALU3", "Z3", "Z3", "AUU1", "AUU0", "Z2", "Z2", "ALL4", "R0", "R1", "ALU4", "R0", "R0", "Z3", "Z3",
    "R1", "R1", "AUU2", "Z2", "Z2", "R0", "R0", "R1", "R1", "Z3", "Z3", "AUU3", "AUU4", "R0", "R2", "R3",
    "R2", "R2", "R3", "R3", "R0", "R1", "R2", "R2", "R3", "R3", "R1", "R2", "R3", "R2", "R3",
)
LAG = 40
LAST = 7
QSCALE = math.log2(math.e) / math.sqrt(HD)
N_SEM = 256


def kernel(mod_ref, tok_in, gain_ref, w_in, hg_ref, w_out, out_ref,
           tok, wcat, wo, acc, ssq, qbuf, kv, o_acc, l_acc, att, term,
           abuf, r1, r2, msg, ubuf, r4, fin, fin_in,
           send_sem, recv_sem, loc_sem):
    m = lax.axis_index("mod")
    z = lax.axis_index("seq")
    tp = lax.axis_index("tp")
    sib = 1 - m
    sa = 4 - 3 * m
    sb = 1 + 3 * m
    a = lax.rem(lax.div(tp, sa), 4)
    b = lax.rem(lax.div(tp, sb), 4)

    def slot(i, k):
        return lax.rem(a + i, 4) * sa + lax.rem(b + k, 4) * sb

    a_next, a_prev = {"tp": slot(1, 0)}, {"tp": slot(3, 0)}
    b_next, b_prev = {"tp": slot(0, 1)}, {"tp": slot(0, 3)}
    a_far, b_far = {"tp": slot(2, 0)}, {"tp": slot(0, 2)}
    z_next, z_prev = {"seq": lax.rem(z + 1, 8)}, {"seq": lax.rem(z + 7, 8)}
    other = {"mod": sib}

    barrier = pltpu.get_barrier_semaphore()
    for dev in (a_next, a_prev, a_far, b_next, b_prev, b_far, z_next, z_prev, other):
        pl.semaphore_signal(barrier, inc=1, device_id=dev, device_id_type=MESH)
    tme = slot(0, 0)
    own_copies, w_local, wo_local, wo_remote = [], [], [], []
    for h in range(NH):
        cp = pltpu.make_async_copy(tok_in.at[pl.ds(h * R, R), :], tok.at[m * NH + h, tme], loc_sem.at[h])
        cp.start()
        own_copies.append(cp)
    for p in range(3):
        cp = pltpu.make_async_copy(
            w_in.at[p, :, pl.ds(pl.multiple_of(m * HD, HD), HD)],
            wcat.at[:, pl.ds(p * HD, HD)], loc_sem.at[NH + p])
        cp.start()
        w_local.append(cp)
    for i in range(4):
        for k in range(4):
            t = i * sa + k * sb
            cp = pltpu.make_async_copy(
                w_out.at[:, pl.ds(pl.multiple_of(t * W + m * HD, HD), HD)],
                wo.at[i, pl.ds(0, 256), pl.ds(k * HD, HD)], loc_sem.at[NH + 3 + i * 4 + k])
            cp.start()
            wo_local.append(cp)
    o_acc[...] = jnp.zeros_like(o_acc)
    l_acc[...] = jnp.zeros_like(l_acc)
    pl.semaphore_wait(barrier, 9)


    sent = []
    count = [0]

    def send(src, dst, dev):
        i = count[0]
        count[0] += 1
        copy = pltpu.make_async_remote_copy(
            src_ref=src, dst_ref=dst, send_sem=send_sem.at[i], recv_sem=recv_sem.at[i],
            device_id=dev, device_id_type=MESH)
        copy.start()
        sent.append(copy)
        return copy

    landed = set()

    def arrive(*copies):
        for copy in copies:
            if id(copy) not in landed:
                landed.add(id(copy))
                copy.wait_recv()

    def span_mod(c, block):
        s, h = divmod(c, NH)
        return mod_ref[(s * 8 + z) * TOK + h * R + block * SPAN]

    def pick(flag, one, zero):
        return jnp.where(jnp.full(one.shape, flag, jnp.int32) == 1, one, zero)

    swap = []
    w_remote = []
    for h in range(NH):
        swap.append(send(tok_in.at[pl.ds(h * R, R), :], tok.at[m * NH + h, tme], other))
    for p in range(3):
        w_remote.append(send(
            w_in.at[p, :, pl.ds(pl.multiple_of(sib * HD, HD), HD)],
            wcat.at[:, pl.ds(384 + p * HD, HD)], other))

    hops = {}

    def gather(c):
        rows = pl.ds(pl.multiple_of(m * H, H), H)
        low = pl.ds(pl.multiple_of(m * H, Q4), Q4)
        high = pl.ds(pl.multiple_of(m * H + Q4, Q4), Q4)

        def put(t, part, dev):
            ref = tok.at[c, t, part]
            return send(ref, ref, dev)

        own = slot(0, 0)
        ar = put(own, rows, a_next)
        al = put(own, rows, a_prev)
        af = put(own, rows, a_far)
        bn, bp = {}, {}
        d2d = hops[c] = {}
        bn[0] = put(own, rows, b_next)
        bp[0] = put(own, rows, b_prev)
        yield
        arrive(ar)
        bn[3] = put(slot(3, 0), rows, b_next)
        bp[3] = put(slot(3, 0), rows, b_prev)
        d2d[3, 0] = put(slot(3, 0), rows, other)
        yield
        arrive(al)
        bn[1] = put(slot(1, 0), rows, b_next)
        bp[1] = put(slot(1, 0), rows, b_prev)
        d2d[1, 0] = put(slot(1, 0), rows, other)
        yield
        arrive(af)
        bn[2] = put(slot(2, 0), rows, b_next)
        bp[2] = put(slot(2, 0), rows, b_prev)
        d2d[2, 0] = put(slot(2, 0), rows, other)
        yield
        g1, g2 = {}, {}
        for i in (0, 3, 1, 2):
            arrive(bn[i])
            g1[i] = put(slot(i, 3), low, b_next)
            d2d[i, 3] = put(slot(i, 3), rows, other)
            arrive(bp[i])
            g2[i] = put(slot(i, 1), high, b_prev)
            d2d[i, 1] = put(slot(i, 1), rows, other)
            yield
        for i in (0, 3, 1, 2):
            arrive(g1[i], g2[i])
            d2d[i, 2] = put(slot(i, 2), rows, other)
            yield

    def scaled_slice(c, t):
        x = tok[c, t]
        g = gain_ref[:, pl.ds(pl.multiple_of(t * W, W), W)]
        scaled, squares = [], []
        for k in range(R // SPAN):
            flag = span_mod(c, k)
            xb = x[k * SPAN:(k + 1) * SPAN].astype(F32)
            sq = xb * xb
            squares.append(sq[:, :128] + sq[:, 128:])
            scaled.append((xb * pick(flag, g[1:2], g[0:1])).astype(BF16))
        return jnp.concatenate(squares, axis=0), jnp.concatenate(scaled, axis=0)

    def unit(c, *slots):
        parts = [scaled_slice(c, t) for t in slots]
        rows = [wcat[pl.ds(pl.multiple_of(t * W, W), W), :] for t in slots]
        squares = parts[0][0]
        for part in parts[1:]:
            squares = squares + part[0]
        lhs = jnp.concatenate([part[1] for part in parts], axis=1)
        return squares, jnp.dot(lhs, jnp.concatenate(rows, axis=0), preferred_element_type=F32)

    def units(c, n, where):
        def two(q, carry):
            squares, part = unit(c, slot(*where(2 * q)), slot(*where(2 * q + 1)))
            ssq[c] += squares
            acc[c] += part
            return carry
        lax.fori_loop(0, n // 2, two, 0)
        if n % 2:
            squares, part = unit(c, slot(*where(n - 1)))
            ssq[c] += squares
            acc[c] += part

    def project(c):
        ssq[c], acc[c] = unit(c, slot(0, 0))
        yield
        d2d = hops[c]
        near = [(i, k) for i in (0, 1, 3) for k in (0, 1, 3) if (i, k) != (0, 0)]

        def grid9(q):
            i, k = lax.div(q, 3), lax.rem(q, 3)
            return i + lax.div(i, 2), k + lax.div(k, 2)

        arrive(*[d2d[p] for p in near])
        units(c, 4, lambda q: grid9(q + 1))
        yield
        units(c, 4, lambda q: grid9(q + 5))
        yield
        arrive(*[d2d[i, k] for i in range(4) for k in range(4) if 2 in (i, k)])
        units(c, 4, lambda q: (2, q))
        yield
        units(c, 3, lambda q: (q + lax.div(q, 2), 2))
        yield
        finish_qkv(c)
        yield

    def finish_qkv(c):
        def step(k, carry):
            r0 = pl.multiple_of(k * SPAN, SPAN)
            flag = span_mod(c, k)
            mine = (jnp.full((SPAN, 3 * HD), flag, jnp.int32) == m)
            block = acc[c, pl.ds(r0, SPAN), :]
            block = jnp.where(mine, block[:, :3 * HD], block[:, 3 * HD:])
            mean = jnp.sum(ssq[c, pl.ds(r0, SPAN), :], axis=1, keepdims=True) * (1.0 / D)
            block = block * lax.rsqrt(mean + epsilon)
            qp, kp, vp = block[:, :HD], block[:, HD:2 * HD], block[:, 2 * HD:]
            qg = pick(flag, hg_ref[1, 0:1], hg_ref[0, 0:1])
            kg = pick(flag, hg_ref[1, 1:2], hg_ref[0, 1:2])
            qm = jnp.mean(qp * qp, axis=1, keepdims=True)
            km = jnp.mean(kp * kp, axis=1, keepdims=True)
            qbuf[pl.ds(c * R + r0, SPAN), :] = (qp * lax.rsqrt(qm + epsilon) * (qg * QSCALE)).astype(BF16)
            kv[c // NH, z, pl.ds(c % NH * R + r0, SPAN), 0:HD] = (kp * lax.rsqrt(km + epsilon) * kg).astype(BF16)
            kv[c // NH, z, pl.ds(c % NH * R + r0, SPAN), HD:2 * HD] = vp.astype(BF16)
            return carry
        lax.fori_loop(0, R // SPAN, step, 0)

    ring = {}

    def zring(c):
        def put(src_z, first, count, dev):
            ref = kv.at[c // NH, lax.rem(src_z, 8), pl.ds(c % NH * R + first, count)]
            return send(ref, ref, dev)

        ring[c, "r", 1] = put(z, 0, R, z_next)
        ring[c, "l", 1] = put(z, 0, R, z_prev)
        yield
        for d in (1, 2, 3):
            count = R if d < 3 else R // 2
            arrive(ring[c, "r", d])
            ring[c, "r", d + 1] = put(z + 8 - d, 0, count, z_next)
            yield
            arrive(ring[c, "l", d])
            ring[c, "l", d + 1] = put(z + d, R - count, count, z_prev)
            yield

    def tile(shard, src, r0, diagonal):
        rows = pl.ds(r0, TQ)
        s = lax.dot_general(qbuf[rows, :], kv[shard, src, :, 0:HD], (((1,), (1,)), ((), ())),
                            preferred_element_type=F32)
        p = jnp.exp2(s)
        if diagonal:
            at = lax.broadcasted_iota(jnp.int32, p.shape, 0) + (r0 - shard * TOK)
            p = jnp.where(lax.broadcasted_iota(jnp.int32, p.shape, 1) <= at, p, 0.0)
        total = p[:, 0:128]
        for k in range(1, TOK // 128):
            total = total + p[:, k * 128:(k + 1) * 128]
        l_acc[rows, :] += total
        o_acc[rows, :] += jnp.dot(p.astype(BF16), kv[shard, src, :, HD:2 * HD], preferred_element_type=F32)

    half = TOK // TQ

    def attend(shard, target, d):
        first = target * half
        if d == 0:
            def own(n, carry):
                tile(shard, z, pl.multiple_of(n * TQ, TQ), shard == target)
                return carry
            lax.fori_loop(first, first + half, own, 0)
            return
        for h in range(NH):
            arrive(ring[shard * NH + h, "r", d], ring[shard * NH + h, "l", d])

        def side(q, carry):
            src = lax.rem(z + 8 - d + q * 2 * d, 8)

            def step(n, inner):
                tile(shard, src, pl.multiple_of(n * TQ, TQ), False)
                return inner
            seen = first + half if shard < target else jnp.where(src < z, first + half, first)
            lax.fori_loop(first, seen, step, 0)
            return carry
        lax.fori_loop(0, 2 if d < 4 else 1, side, 0)

    low_half = pl.ds(0, R // 2)
    high_half = pl.ds(R // 2, R // 2)

    def reduce(c):
        rows = pl.ds(c * R, R)
        total = jnp.sum(l_acc[rows, :], axis=1, keepdims=True)
        att[c, m] = (o_acc[rows, :] / total).astype(BF16)
        ref = att.at[c, m]
        swapped = send(ref, ref, other)
        yield
        arrive(swapped)

        zero = jnp.zeros((SPAN, HD), BF16)
        for n in range(R // SPAN):
            mine = (jnp.full((SPAN, HD), span_mod(c, n), jnp.int32) == m)
            for h in range(2):
                part = att[c, h, n * SPAN:(n + 1) * SPAN, :]
                abuf[c, n * SPAN:(n + 1) * SPAN, h * HD:(h + 1) * HD] = jnp.where(mine, part, zero)
                abuf[c, n * SPAN:(n + 1) * SPAN, 256 + h * HD:256 + (h + 1) * HD] = jnp.where(mine, zero, part)

        def product(g):
            res = jnp.dot(abuf[c], wo[lax.rem(a + g, 4)], preferred_element_type=F32).astype(BF16)
            for k4 in range(4):
                term[c, g, k4] = res[:, k4 * 128:(k4 + 1) * 128]

        product(2)
        s1 = send(term.at[c, 2, :, low_half], r1.at[c, 0], a_next)
        s2 = send(term.at[c, 2, :, high_half], r1.at[c, 1], a_prev)
        yield

        def rest(n, carry):
            product(jnp.where(n == 2, 0, 2 * n + 1))
            return carry
        lax.fori_loop(0, 3, rest, 0)
        yield

        def add(x, y):
            return (x.astype(F32) + y.astype(F32)).astype(BF16)

        arrive(s1)
        msg[c, 0, :, low_half] = add(term[c, 1, :, low_half], r1[c, 0])
        msg[c, 0, :, high_half] = term[c, 1, :, high_half]
        s3 = send(msg.at[c, 0], r2.at[c, 0], a_next)
        yield
        arrive(s2)
        msg[c, 1, :, high_half] = add(term[c, 3, :, high_half], r1[c, 1])
        msg[c, 1, :, low_half] = term[c, 3, :, low_half]
        s4 = send(msg.at[c, 1], r2.at[c, 1], a_prev)
        yield
        arrive(s3, s4)

        def total4(k, carry):
            ubuf[c, k] = (term[c, 0, k].astype(F32) + r2[c, 0, k].astype(F32)
                          + r2[c, 1, k].astype(F32)).astype(BF16)
            return carry

        reach = []
        for k, (i, dev) in enumerate(((2, b_far), (1, b_next), (3, b_prev))):
            to = lax.rem(b + i, 4)
            total4(to, 0)
            reach.append(send(ubuf.at[c, to], r4.at[c, k], dev))
        total4(b, 0)
        yield
        arrive(*reach)
        fin[c] = (ubuf[c, b].astype(F32) + r4[c, 0].astype(F32) + r4[c, 1].astype(F32)
                  + r4[c, 2].astype(F32)).astype(BF16)
        yield

    streams = {}
    for c in range(2 * NH):
        streams["G%d" % c] = gather(c)
        streams["Q%d" % c] = project(c)
        streams["Z%d" % c] = zring(c)
        streams["R%d" % c] = reduce(c)

    seen = set()
    issued = []
    turns = {}
    back = {}
    retired = 0
    for number, name in enumerate(ORDER):
        issued.append(len(sent))
        if number >= LAG:
            while retired < issued[number - LAG]:
                sent[retired].wait_send()
                retired += 1
        if name[0] == "A":
            attend("LU".index(name[1]), "LU".index(name[2]), int(name[3]))
            continue
        if name[0] in "GQ" and ("own", int(name[1]) % NH) not in seen:
            h = int(name[1]) % NH
            seen.add(("own", h))
            own_copies[h].wait()
            arrive(swap[h])
        if name[0] == "Q" and "Q" not in seen:
            seen.add("Q")
            for cp in w_local:
                cp.wait()
            arrive(*w_remote)
        if name == "Z0" and "Z" not in seen:
            seen.add("Z")
            for i in range(4):
                for k in range(4):
                    t = i * sb + k * sa
                    wo_remote.append(send(
                        w_out.at[:, pl.ds(pl.multiple_of(t * W + sib * HD, HD), HD)],
                        wo.at[i, pl.ds(256, 256), pl.ds(k * HD, HD)], other))
        if name[0] == "R" and "R" not in seen:
            seen.add("R")
            for cp in wo_local:
                cp.wait()
            arrive(*wo_remote)
        next(streams[name])
        if name[0] == "R":
            turns[name] = turns.get(name, 0) + 1
            h = int(name[1]) % NH
            if turns.get("R%d" % h) == LAST and turns.get("R%d" % (h + NH)) == LAST:
                back[h] = send(fin.at[sib * NH + h], fin_in.at[h], other)

    for h in range(NH):
        arrive(back[h])
        own = fin[m * NH + h]
        got = fin_in[h]
        lower = jnp.full(own.shape, m, jnp.int32) == 0
        out_ref[h * R:(h + 1) * R, 0:HD] = jnp.where(lower, own, got)
        out_ref[h * R:(h + 1) * R, HD:2 * HD] = jnp.where(lower, got, own)
    for cp in sent[retired:]:
        cp.wait_send()


def body(tokens, modality, norm_gain, input_weight, head_gain, output_weight):
    chunks = 2 * NH
    vmem = pl.BlockSpec(memory_space=pltpu.VMEM)
    anywhere = pl.BlockSpec(memory_space=pl.ANY)
    w3 = jnp.transpose(input_weight[0], (1, 0, 2))
    return pl.pallas_call(
        kernel,
        out_shape=jax.ShapeDtypeStruct((TOK, W), BF16),
        in_specs=[pl.BlockSpec(memory_space=pltpu.SMEM), vmem, vmem, anywhere, vmem, anywhere],
        out_specs=vmem,
        scratch_shapes=[
            pltpu.VMEM((chunks, 16, R, W), BF16),
            pltpu.VMEM((D, 6 * HD), BF16),
            pltpu.VMEM((4, 512, 512), BF16),
            pltpu.VMEM((chunks, R, 6 * HD), F32),
            pltpu.VMEM((chunks, R, 128), F32),
            pltpu.VMEM((2 * TOK, HD), BF16),
            pltpu.VMEM((2, 8, TOK, 2 * HD), BF16),
            pltpu.VMEM((2 * TOK, HD), F32),
            pltpu.VMEM((2 * TOK, 128), F32),
            pltpu.VMEM((chunks, 2, R, HD), BF16),
            pltpu.VMEM((chunks, 4, 4, R, 128), BF16),
            pltpu.VMEM((chunks, R, 512), BF16),
            pltpu.VMEM((chunks, 2, 4, R // 2, 128), BF16),
            pltpu.VMEM((chunks, 2, 4, R, 128), BF16),
            pltpu.VMEM((chunks, 2, 4, R, 128), BF16),
            pltpu.VMEM((chunks, 4, R, 128), BF16),
            pltpu.VMEM((chunks, 3, R, 128), BF16),
            pltpu.VMEM((chunks, R, 128), BF16),
            pltpu.VMEM((NH, R, 128), BF16),
            pltpu.SemaphoreType.DMA((N_SEM,)),
            pltpu.SemaphoreType.DMA((N_SEM,)),
            pltpu.SemaphoreType.DMA((NH + 3 + 16,)),
        ],
        compiler_params=pltpu.CompilerParams(
            collective_id=0, has_side_effects=True, vmem_limit_bytes=56 * 1024 * 1024),
    )(modality, tokens, norm_gain, w3, head_gain, output_weight[0])


def solution(mesh):
    in_specs = (
        P(("mod", "seq"), "tp"),
        P(),
        P(),
        P("mod", None, None, "tp"),
        P(),
        P("mod", "tp", None),
    )
    out_specs = P(("mod", "seq"), "tp")
    return jax.shard_map(body, mesh=mesh, in_specs=in_specs, out_specs=out_specs, check_vma=False)
```
